32 devices in a mesh: clip: 4 (over y, core), tm: 2 (over x), space: 4 (over z).
Axes of the slice: x: 2, y: 2, z: 4, core: 2. Of those that a mesh axis runs over, the one named last changes fastest.
Arguments:
- video: bfloat16 [4, 8, 24, 160, 128], P('clip', 'tm', 'space'), may hold values from -6 to 6
- frame_counts: int32 [4], P('clip'), may hold values from 2 to 8, as said below
- conv_weight: bfloat16 [3, 3, 3, 128, 128], replicated, may hold values from -0.109375 to 0.109375
- norm_gain: float32 [128], replicated, may hold values from 0.25 to 1.75
- norm_shift: float32 [128], replicated, may hold values from -3 to 3
- quant_weight: bfloat16 [128, 32], replicated, may hold values from -0.5 to 0.5
- quant_bias: float32 [32], replicated, may hold values from -3 to 3
- row_dest: int32 [4, 2, 4, 24, 1], P('clip', 'tm', 'space'), may hold values from 0 to 1; in each aligned block of 24 rows (0 to 23, 24 to 47, ..., all dimensions but the last counted through in order) at most 24 rows name the same one
Outputs:
- latent_shards: bfloat16 [4, 2, 4, 2, 24, 5120], P('clip', 'tm', 'space')
The draws below stay inside these ranges and needn't reach their ends.
Inputs may be any that keep to these rules, and one draw needn't show every extreme that they name: `frame_counts`: every clip has at least one valid frame; some clip has all 8 frames valid. `row_dest`: among the 24 rows of one device, no sequence shard is named by more than 24 rows.
All inputs are finite; a program needn't handle non-finite values.
Results may differ from the reference program's by a relative error of at most 0.0037.
The reference program's roundings to bfloat16 on the way (of `masked`, `padded`, `hidden` and `moments`) count: a program that leaves them out, or rounds other values in their place, can miss the bound.
Values may be sent and summed in bfloat16 or wider, within the bound.
A program may use at most 64 MiB of HBM per device.

```python
import math
import jax
import jax.numpy as jnp
import numpy as np
from jax import lax

C = 128
GROUPS = 32
F_DEV = 4
H_DEV = 6
W = 160
L2 = 32
G = 4
F = 8
H = 24
R = 24
CAP = 24
N_TM = 2
N_SPACE = 4


def draw_frame_counts(key, part):
    counts = jax.random.randint(key, (G,), max(1, F // 4), F + 1)
    pick = jax.random.randint(jax.random.fold_in(key, 7), (), 0, G)
    return jnp.where(jnp.arange(G) == pick, F, counts).astype(jnp.int32)


def levels(key, shape, pieces, least, largest):
    loudness, own = 1.0, jax.random.fold_in(key, 6)
    for dim, parts in pieces:
        draws = jnp.exp(jax.random.uniform(jax.random.fold_in(own, dim), (parts,), jnp.float32, least / len(pieces), largest / len(pieces)))
        loudness = loudness * jnp.repeat(draws, shape[dim] // parts).reshape([-1 if axis == dim else 1 for axis in range(len(shape))])
    return loudness


def shared_out(own_key, own, number, rows, amount, top, reach, lean):
    order = jax.random.permutation(own_key, amount)
    packed, ordinary = shares(amount, rows * top, reach, lean, True), shares(amount, rows * top, reach, lean, False)
    places = jnp.arange(amount)

    def named(sizes, rotation):
        used = int((sizes > 0).sum())
        fixed = max(1, used // 4)
        passed = fixed + (places - fixed + rotation * (used - fixed)) % max(1, amount - fixed)
        return jnp.zeros((amount,), jnp.int32).at[order[jnp.where(places < fixed, places, passed)]].set(jnp.asarray(sizes, jnp.int32))

    sizes = jnp.where(number % 4 == 0, named(packed, number // 4), named(ordinary, number - number // 4 - 1))
    mixed = jax.random.permutation(jax.random.fold_in(own, 3), amount)
    giver, sink = mixed[0:amount // 2 * 2:2], mixed[1:amount // 2 * 2:2]
    room = jnp.minimum(sizes[giver] - 1, reach - sizes[sink]) // 2
    room = jnp.where((giver == order[0]) | (sink == order[0]) | (sizes[sink] == 0), 0, jnp.maximum(room, 0))
    passed = jax.random.randint(jax.random.fold_in(own, 4), (amount // 2,), 0, 1 << 20) % (room + 1)
    sizes = sizes.at[giver].add(-passed).at[sink].add(passed)
    members = jnp.searchsorted(jnp.cumsum(sizes), jnp.arange(rows * top), side="right").astype(jnp.int32)
    grid = members.reshape(top, rows).T
    grid = grid[jax.random.permutation(jax.random.fold_in(own, 1), rows)]
    rotation = jax.random.randint(jax.random.fold_in(own, 2), (rows, 1), 0, top)
    return jnp.take_along_axis(grid, (jnp.arange(top)[None, :] + rotation) % top, axis=1)


def shares(number_of, total, limit, slope, full):
    loads = [(1 << 20) // math.isqrt(standing ** slope) + 1 for standing in range(1, number_of + 1)]
    largest = limit if full else min(limit, max(-(-total // number_of), total * loads[0] // sum(loads)))
    least = 1 if total - largest >= number_of - 1 else 0
    holding, surplus = [largest] + [least] * (number_of - 1), total - largest - least * (number_of - 1)
    while surplus > 0:
        movable = [i for i in range(1, number_of) if holding[i] < largest] or [i for i in range(1, number_of) if holding[i] < limit]
        pool, budget = sum([loads[i] for i in movable]), surplus
        for i in movable:
            extra = min(limit - holding[i], max(1, budget * loads[i] // pool), surplus)
            holding[i] = holding[i] + extra
            surplus = surplus - extra
    return np.array(holding)


def centred(rng, extent, scale, limit, shards=(), kind=jnp.bfloat16):
    values = jax.random.normal(rng, extent, jnp.float32) * scale
    if len(shards) > 0:
        values = levels(rng, extent, shards, -0.22, 0.18) * values
    return jnp.clip(values, min=-limit, max=limit).astype(kind)


def setup_inputs(seed: int = 0) -> dict:
    key_list = jax.random.split(jax.random.key(seed), 9)
    video = centred(key_list[0], (G, F, H, W, C), 1.0, 6.0, ((0, 4), (1, 2), (2, 4)))
    frame_counts = draw_frame_counts(jax.random.fold_in(key_list[8], 71), 0)
    conv_weight = centred(key_list[2], (3, 3, 3, C, C), (27 * C) ** -0.5, 0.109375)
    norm_gain = jnp.clip(1.0 + 0.15 * jax.random.normal(key_list[3], (C,), jnp.float32), 0.25, 1.75)
    norm_shift = centred(key_list[4], (C,), 0.5, 3.0, (), jnp.float32)
    quant_weight = centred(key_list[5], (C, L2), C ** -0.5, 0.5)
    quant_bias = centred(key_list[6], (L2,), 0.5, 3.0, (), jnp.float32)
    row_dest_keys = jax.random.split(jax.random.fold_in(key_list[7], 1), G * N_TM * N_SPACE * R // R)
    row_dest_turns = jax.random.permutation(jax.random.fold_in(key_list[7], 3), G * N_TM * N_SPACE * R // R)
    row_dest = jax.vmap(lambda own, number: shared_out(jax.random.fold_in(key_list[7], 2), own, number, R, N_TM, 1, CAP, 2))(row_dest_keys, row_dest_turns).reshape((G, N_TM, N_SPACE, R, 1))
    return {"video": video, "frame_counts": frame_counts, "conv_weight": conv_weight, "norm_gain": norm_gain, "norm_shift": norm_shift, "quant_weight": quant_weight, "quant_bias": quant_bias, "row_dest": row_dest}


def conv_clip(masked_clip, conv_weight):
    first = masked_clip[:1]
    timed = jnp.concatenate([first, first, masked_clip], axis=0)
    padded = jnp.pad(timed, ((0, 0), (1, 1), (1, 1), (0, 0)))
    frames = masked_clip.shape[0]
    rows = masked_clip.shape[1]
    cells = masked_clip.shape[2]
    chans = masked_clip.shape[3]
    total = jnp.zeros((frames * rows * cells, chans), jnp.float32)
    for dh in range(3):
        for dw in range(3):
            window = padded[:, dh:dh + rows, dw:dw + cells, :]
            stacked = jnp.concatenate([window[dt:dt + frames] for dt in range(3)], axis=3)
            kernel = conv_weight[:, dh, dw].reshape(3 * chans, chans)
            total = total + jnp.dot(stacked.reshape(-1, 3 * chans), kernel, preferred_element_type=jnp.float32)
    return total.reshape(frames, rows, cells, chans)

def encode_clip(inputs, conv_weight, norm_gain, norm_shift, quant_weight, quant_bias):
    clip_video, count = inputs
    valid = (jnp.arange(F, dtype=jnp.int32) < count).astype(jnp.float32)
    masked = clip_video * valid.astype(jnp.bfloat16)[:, None, None, None]
    act = conv_clip(masked, conv_weight) * valid[:, None, None, None]
    per = C // GROUPS
    grouped = act.reshape(F, H, W, GROUPS, per)
    total_count = count.astype(jnp.float32) * (H * W * per)
    mean = lax.optimization_barrier(jnp.sum(grouped, axis=(0, 1, 2, 4))) / total_count
    centered = (grouped - mean[:, None]) * valid[:, None, None, None, None]
    var = lax.optimization_barrier(jnp.sum(centered * centered, axis=(0, 1, 2, 4))) / total_count
    normed = ((grouped - mean[:, None]) / jnp.sqrt(var[:, None] + 1e-06)).reshape(F, H, W, C)
    normed = normed * norm_gain + norm_shift
    hidden = (jax.nn.silu(normed) * valid[:, None, None, None]).astype(jnp.bfloat16)
    moments = jnp.dot(hidden.reshape(-1, C), quant_weight, preferred_element_type=jnp.float32) + quant_bias
    moments = moments.astype(jnp.bfloat16).reshape(N_TM, F_DEV, N_SPACE, H_DEV, W * L2)
    return jnp.transpose(moments, (0, 2, 1, 3, 4)).reshape(N_TM, N_SPACE, R, W * L2)

def route_clip(inputs):
    rows, dest = inputs
    onehot = (dest[..., None] == jnp.arange(N_TM, dtype=jnp.int32)).astype(jnp.int32)
    before = jnp.cumsum(onehot, axis=2) - onehot
    rank = lax.optimization_barrier(jnp.sum(before * onehot, axis=3))
    slot = dest * CAP + rank
    place = (slot[..., None] == jnp.arange(N_TM * CAP, dtype=jnp.int32)).astype(jnp.float32)
    send = jnp.einsum('tsrq,tsrv->tsqv', place, rows.astype(jnp.float32))
    send = send.reshape(N_TM, N_SPACE, N_TM, CAP, W * L2)
    return jnp.transpose(send, (2, 1, 0, 3, 4)).astype(jnp.bfloat16)

def reference(video, frame_counts, conv_weight, norm_gain, norm_shift, quant_weight, quant_bias, row_dest):
    encode = lambda inputs: encode_clip(inputs, conv_weight, norm_gain, norm_shift, quant_weight, quant_bias)
    rows = lax.map(encode, (video, frame_counts))
    return lax.map(route_clip, (rows, row_dest[..., 0]))
```

```python
import functools

import jax
import jax.numpy as jnp
from jax import lax
from jax.experimental import pallas as pl
from jax.experimental.pallas import tpu as pltpu
from jax.sharding import PartitionSpec as P

GROUPS = 32
MESH = pl.DeviceIdType.MESH
TILES = 8
VMEM = 64 * 1024 * 1024


def kernel(
    n_tm,
    n_space,
    cap,
    capb,
    slots_per,
    pitch,
    count_hbm,
    video,
    weight,
    gain_hbm,
    shift_hbm,
    qw_hbm,
    qb_hbm,
    dest_hbm,
    out,
    count_ref,
    gain_ref,
    shift_ref,
    qw_ref,
    qb_ref,
    dest_ref,
    next_ref,
    xs,
    wb,
    act,
    wq,
    place,
    stats,
    gathered,
    outgoing,
    local_sem,
    halo_send,
    halo_recv,
    stat_send,
    stat_recv,
    row_send,
    row_recv,
    own_sem,
):
    fdev, hdev, width, chans = video.shape
    l2 = qw_ref.shape[0]
    rows = fdev * hdev
    held = place.shape[1]
    folded = chans // l2
    lat = width * l2
    n = n_tm * n_space
    tm, space = lax.axis_index("tm"), lax.axis_index("space")
    me = tm * n_space + space
    first_tm, last_tm = tm == 0, tm == n_tm - 1

    def at(peer):
        return {"tm": peer // n_space, "space": lax.rem(peer, n_space)}

    barrier = pltpu.get_barrier_semaphore()

    @pl.loop(1, n)
    def _(step):
        pl.semaphore_signal(
            barrier, inc=1, device_id=at(lax.rem(me + step, n)), device_id_type=MESH
        )

    own = pltpu.make_async_copy(
        video, xs.at[pl.ds(1, fdev), pl.ds(1, hdev)], local_sem.at[0]
    )
    own.start()
    taps = [
        pltpu.make_async_copy(
            weight.at[:, :, dw],
            wb.at[:, :, :, pl.ds(dw * chans, chans)],
            local_sem.at[1 + dw],
        )
        for dw in range(3)
    ]
    for tap in taps:
        tap.start()

    smalls = [
        pltpu.make_async_copy(src, dst, local_sem.at[4 + i])
        for i, (src, dst) in enumerate(
            [
                (qw_hbm, qw_ref),
                (qb_hbm, qb_ref),
                (dest_hbm, dest_ref),
                (gain_hbm, gain_ref),
                (shift_hbm, shift_ref),
                (count_hbm, count_ref),
            ]
        )
    ]
    for small in smalls:
        small.start()

    pl.semaphore_wait(barrier, n - 1)

    def remote(src, dst, index, device):
        return pltpu.make_async_remote_copy(
            src_ref=src,
            dst_ref=dst,
            send_sem=halo_send.at[index],
            recv_sem=halo_recv.at[index],
            device_id=device,
            device_id_type=MESH,
        )

    later = {"tm": lax.rem(tm + 1, n_tm)}
    earlier = {"tm": lax.rem(tm + n_tm - 1, n_tm)}
    above = {"space": lax.rem(space + n_space - 1, n_space)}
    below = {"space": lax.rem(space + 1, n_space)}
    after = fdev + 1

    def frame_copies(source, target, index, device):
        return [
            remote(video.at[source, 0], xs.at[target, 1], index, device),
            remote(video.at[source, hdev - 1], xs.at[target, hdev], index + 1, device),
            remote(
                video.at[source, pl.ds(1, hdev - 2)],
                xs.at[target, pl.ds(2, hdev - 2)],
                index + 2,
                device,
            ),
        ]

    def corner_copies(target, index):
        return [
            remote(xs.at[target, 1], xs.at[target, hdev + 1], index, above),
            remote(xs.at[target, hdev], xs.at[target, 0], index + 1, below),
        ]

    forward = frame_copies(fdev - 1, 0, 0, later)
    back = frame_copies(0, after, 3, earlier)
    forward_corners = corner_copies(0, 6)
    back_corners = corner_copies(after, 8)
    up = remote(video.at[:, 0], xs.at[pl.ds(1, fdev), hdev + 1], 10, above)
    down = remote(video.at[:, hdev - 1], xs.at[pl.ds(1, fdev), 0], 11, below)
    dest_copy = remote(dest_hbm, next_ref, 12, earlier)

    @pl.when(tm < n_tm - 1)
    def _():
        for copy in forward:
            copy.start()

    @pl.when(tm > 0)
    def _():
        for copy in back:
            copy.start()

    @pl.when(space > 0)
    def _():
        up.start()

    @pl.when(space < n_space - 1)
    def _():
        down.start()

    @pl.when(tm > 0)
    def _():
        dest_copy.start()

    zero_row = jnp.zeros((fdev + 2, width, chans), jnp.bfloat16)

    @pl.when(space == 0)
    def _():
        xs[:, 0] = zero_row

    @pl.when(space == n_space - 1)
    def _():
        xs[:, hdev + 1] = zero_row

    zero_frame = jnp.zeros((hdev * pitch, chans), jnp.float32)

    @pl.when(tm > 0)
    def _():
        act[pl.ds(0, hdev * pitch), :] = zero_frame

    @pl.when(tm == n_tm - 1)
    def _():
        act[pl.ds(rows * pitch, hdev * pitch), :] = zero_frame

    spare = held - rows - hdev
    act[pl.ds((rows + hdev) * pitch, spare * pitch), :] = jnp.zeros(
        (spare * pitch, chans), jnp.float32
    )

    for small in smalls:
        small.wait()
    lane = lax.broadcasted_iota(jnp.int32, (l2, chans), 1)
    sub = lax.broadcasted_iota(jnp.int32, (l2, chans), 0)
    spread = jnp.zeros((l2, chans), jnp.float32)
    for i in range(folded):
        pick = jnp.where(lane == sub + i * l2, 1.0, 0.0)
        spread = spread + pick
        wq[pl.ds(i * chans, chans), :] = lax.dot_general(
            qw_ref[...],
            pick.astype(jnp.bfloat16),
            (((0,), (0,)), ((), ())),
            preferred_element_type=jnp.float32,
        ).astype(jnp.bfloat16)
    bias = jnp.dot(
        qb_ref[...],
        spread,
        precision=lax.Precision.HIGHEST,
        preferred_element_type=jnp.float32,
    )
    stats[...] = jnp.zeros_like(stats)

    count = count_ref[...]

    def valid(frame):
        ids = jnp.full((1, chans), 0, jnp.int32) + (tm * fdev + frame)
        return jnp.where(ids < count, 1.0, 0.0)

    cell = lax.broadcasted_iota(jnp.int32, (width, chans), 0)

    def accumulate(fs, taps_of, fresh, final, hs):
        items = [(f, h) for f in fs for h in hs]
        m = len(items) * width

        def index(f, dt):
            p = f - 1 + dt
            return 1 if f == 0 else jnp.where(first_tm, 1, p) if p == 0 else p

        pieces = [
            jnp.concatenate([xs[index(f, dt), h + dh] for f, h in items], axis=0)
            for dt in taps_of
            for dh in range(3)
        ]
        kernel_part = wb[pl.ds(taps_of[0], len(taps_of))].reshape(-1, 3 * chans)
        y = jnp.dot(
            jnp.concatenate(pieces, axis=1), kernel_part, preferred_element_type=jnp.float32
        )
        for i, (f, h) in enumerate(items):
            part = y[i * width : (i + 1) * width]
            before = pltpu.roll(part[:, :chans], 1, 0)
            after_ = pltpu.roll(part[:, 2 * chans :], width - 1, 0)
            total = (
                part[:, chans : 2 * chans]
                + jnp.where(cell == 0, 0.0, before)
                + jnp.where(cell == width - 1, 0.0, after_)
            )
            spot = pl.ds((f * hdev + h) * pitch, width)
            if not fresh:
                total = total + act[spot, :]
            if final:
                total = total * valid(f)
                stats[0] += jnp.sum(total.reshape(width // 8, 8, chans), axis=0)
                stats[1] += jnp.sum((total * total).reshape(width // 8, 8, chans), axis=0)
            act[spot, :] = total

    inner, edge = list(range(1, hdev - 1)), [0, hdev - 1]

    own.wait()
    for tap in taps:
        tap.wait()

    def own_taps(part):
        accumulate(range(2, fdev), (0, 1, 2), True, True, part)
        accumulate([1], (1, 2), True, False, part)

        @pl.when(tm < n_tm - 1)
        def _():
            accumulate([fdev], (0, 1), True, False, part)

        @pl.when(tm == 0)
        def _():
            accumulate([0], (0, 1, 2), True, True, part)

    own_taps(inner)

    def pass_corners(arrived, corners):
        arrived[0].wait_recv()
        arrived[1].wait_recv()

        @pl.when(space > 0)
        def _():
            corners[0].start()

        @pl.when(space < n_space - 1)
        def _():
            corners[1].start()

    @pl.when(tm > 0)
    def _():
        pass_corners(forward, forward_corners)

    @pl.when(tm < n_tm - 1)
    def _():
        pass_corners(back, back_corners)

    @pl.when(space < n_space - 1)
    def _():
        up.wait_recv()

    @pl.when(space > 0)
    def _():
        down.wait_recv()

    own_taps(edge)

    @pl.when(tm < n_tm - 1)
    def _():
        dest_copy.wait_recv()

    @pl.when(tm == n_tm - 1)
    def _():
        next_ref[...] = jnp.zeros_like(next_ref)

    def numbers(shape, axis):
        return lax.broadcasted_iota(jnp.int32, shape, axis)

    along, across = numbers((held, held), 0), numbers((held, held), 1)
    source, column = numbers((rows, held), 0), numbers((rows, held), 1)
    named = jnp.dot(
        dest_ref[...].astype(jnp.float32),
        jnp.where(source == column, 1.0, 0.0),
        precision=lax.Precision.HIGHEST,
        preferred_element_type=jnp.float32,
    ) + jnp.dot(
        next_ref[...].astype(jnp.float32),
        jnp.where((source + rows == column) & (source < hdev), 1.0, 0.0),
        precision=lax.Precision.HIGHEST,
        preferred_element_type=jnp.float32,
    )
    wide_named = jnp.broadcast_to(named, (held, held))
    tall_named = jnp.sum(jnp.where(across == along, wide_named, 0.0), axis=1, keepdims=True)
    alike = (tall_named == wide_named) & (along < across) & ((along < rows) == (across < rows))
    rank = jnp.sum(jnp.where(alike, 1.0, 0.0), axis=0, keepdims=True)
    position = numbers((1, held), 1)
    here = (
        ((position < hdev) & first_tm)
        | ((position >= hdev) & (position < rows))
        | ((position >= rows) & (position < rows + hdev) & (~last_tm))
    )
    slot = named * slots_per + rank + jnp.where(position >= rows, 1.0 * cap, 0.0)
    slot = jnp.where(here, slot, -1.0)
    slots = numbers((place.shape[0], held), 0).astype(jnp.float32)
    place[...] = jnp.where(slots == slot, 1.0, 0.0).astype(jnp.bfloat16)

    def corners_in(corners):
        @pl.when(space < n_space - 1)
        def _():
            corners[0].wait_recv()

        @pl.when(space > 0)
        def _():
            corners[1].wait_recv()

    @pl.when(tm > 0)
    def _():
        corners_in(forward_corners)
        forward[2].wait_recv()

    accumulate([1], (0,), False, True, range(hdev))

    @pl.when(tm < n_tm - 1)
    def _():
        corners_in(back_corners)
        back[2].wait_recv()
        accumulate([fdev], (2,), False, True, range(hdev))

    halves = [jnp.sum(stats[i], axis=0, keepdims=True) for i in range(2)]
    line = lax.broadcasted_iota(jnp.int32, (8, chans), 0)
    gathered[me] = jnp.where(line == 0, halves[0], jnp.where(line == 1, halves[1], 0.0))

    def stat_copy(step):
        return pltpu.make_async_remote_copy(
            src_ref=gathered.at[me],
            dst_ref=gathered.at[me],
            send_sem=stat_send.at[step],
            recv_sem=stat_recv.at[me],
            device_id=at(lax.rem(me + step, n)),
            device_id_type=MESH,
        )

    def stat_arrival(step):
        sender = lax.rem(me + step, n)
        return pltpu.make_async_remote_copy(
            src_ref=gathered.at[sender],
            dst_ref=gathered.at[sender],
            send_sem=stat_send.at[step],
            recv_sem=stat_recv.at[sender],
            device_id=at(sender),
            device_id_type=MESH,
        )

    @pl.loop(1, n)
    def _(step):
        stat_copy(step).start()

    @pl.loop(1, n)
    def _(step):
        stat_arrival(step).wait_recv()

    sums = jnp.sum(gathered[...], axis=0)
    position = lax.broadcasted_iota(jnp.int32, (8, chans), 1)
    per = chans // GROUPS
    reach = 1
    while reach < per:
        low = lax.rem(position // reach, 2) == 0
        sums = sums + jnp.where(
            low, pltpu.roll(sums, chans - reach, 1), pltpu.roll(sums, reach, 1)
        )
        reach *= 2
    amount = jnp.full((1, chans), 1, jnp.int32) * count
    total_count = amount.astype(jnp.float32) * (n_space * hdev * width * per)
    mean = sums[0:1] / total_count
    var = jnp.maximum(sums[1:2] / total_count - mean * mean, 0.0)
    scale = lax.rsqrt(var + 1e-06) * gain_ref[...]
    offset = shift_ref[...] - mean * scale
    scale, offset = 0.5 * scale, 0.5 * offset
    row = numbers((held, chans), 0)
    frame = jnp.zeros((held, chans), jnp.int32) + tm * fdev
    for f in range(1, fdev + 1):
        frame = frame + jnp.where(row >= f * hdev, 1, 0)
    frame_masks = jnp.where(frame < count, 1.0, 0.0)
    chunks = lat // (TILES * chans)

    def row_copy(chunk, step, sender):
        peer = lax.rem(tm + step, n_tm)
        columns = pl.ds(pl.multiple_of(chunk * TILES * chans, TILES * chans), TILES * chans)
        return pltpu.make_async_remote_copy(
            src_ref=outgoing.at[peer, :, columns],
            dst_ref=out.at[peer if sender else tm, :, columns],
            send_sem=row_send.at[chunk, step],
            recv_sem=row_recv.at[chunk, peer if sender else tm],
            device_id={"tm": peer},
            device_id_type=MESH,
        )

    @pl.loop(0, chunks)
    def _(chunk):
        hidden = []
        for j in range(TILES):
            cells = []
            for i in range(folded):
                w = (chunk * TILES + j) * folded + i
                half = act[pl.ds(w, held, stride=pitch), :] * scale + offset
                cells.append((half + half * jnp.tanh(half)) * frame_masks)
            hidden.append(jnp.concatenate(cells, axis=1))
        hidden = jnp.concatenate(hidden, axis=0).astype(jnp.bfloat16)
        moments = jnp.dot(hidden, wq[...], preferred_element_type=jnp.float32) + bias
        wide = jnp.concatenate(
            [moments[j * held : (j + 1) * held] for j in range(TILES)], axis=1
        )
        routed = jnp.dot(
            place[...], wide.astype(jnp.bfloat16), preferred_element_type=jnp.float32
        )
        columns = pl.ds(pl.multiple_of(chunk * TILES * chans, TILES * chans), TILES * chans)
        for d in range(n_tm):
            outgoing[d, :, columns] = routed[
                d * slots_per : d * slots_per + outgoing.shape[1]
            ].astype(jnp.bfloat16)

        @pl.loop(1, n_tm)
        def _(step):
            row_copy(chunk, step, False).start()

    kept = pltpu.make_async_copy(outgoing.at[tm], out.at[tm], own_sem)
    kept.start()

    @pl.loop(1, n)
    def _(step):
        stat_copy(step).wait_send()

    def sent(corners):
        @pl.when(space > 0)
        def _():
            corners[0].wait_send()

        @pl.when(space < n_space - 1)
        def _():
            corners[1].wait_send()

    @pl.when(tm < n_tm - 1)
    def _():
        for copy in forward:
            copy.wait_send()
        sent(back_corners)

    @pl.when(tm > 0)
    def _():
        for copy in back:
            copy.wait_send()
        dest_copy.wait_send()
        sent(forward_corners)

    @pl.when(space > 0)
    def _():
        up.wait_send()

    @pl.when(space < n_space - 1)
    def _():
        down.wait_send()

    @pl.loop(0, chunks)
    def _(chunk):
        @pl.loop(1, n_tm)
        def _(step):
            row_copy(chunk, step, False).wait_send()
            row_copy(chunk, step, True).wait_recv()

    kept.wait()


def merge(cap, capb, received, out):
    n_tm = out.shape[0]
    for t in range(n_tm):
        if t == 0:
            out[0] = received[0, :cap]
        else:
            first = received[t, :capb].astype(jnp.float32)
            out[t, :capb] = (
                first + received[t - 1, cap : cap + capb].astype(jnp.float32)
            ).astype(jnp.bfloat16)
            if cap > capb:
                out[t, capb:] = received[t, capb:cap]


def body(
    n_tm,
    n_space,
    video,
    frame_counts,
    conv_weight,
    norm_gain,
    norm_shift,
    quant_weight,
    quant_bias,
    row_dest,
):
    clips, fdev, hdev, width, chans = video.shape
    l2 = quant_weight.shape[1]
    rows = fdev * hdev
    lat = width * l2
    cap = min(max(2, 2 * rows // n_tm), rows)
    capb = min(cap, hdev)
    sent = cap + capb
    if sent > 16:
        sent = -(-sent // 16) * 16
    slots_per = -(-sent // 8) * 8
    held = -(-(rows + hdev) // 16) * 16
    pitch = width + 8
    n = n_tm * n_space
    chunks = lat // (TILES * chans)
    kept_bytes = n_tm * -(-sent // 16) * 16 * lat * 2 + 64 * 1024
    hbm = pl.BlockSpec(memory_space=pltpu.HBM)
    out = pl.pallas_call(
        functools.partial(kernel, n_tm, n_space, cap, capb, slots_per, pitch),
        out_shape=pltpu.VMEM((n_tm, sent, lat), jnp.bfloat16),
        in_specs=[hbm] * 8,
        out_specs=pl.BlockSpec(memory_space=pl.ANY),
        scratch_shapes=[
            pltpu.VMEM((1, 1), jnp.int32),
            pltpu.VMEM((1, chans), jnp.float32),
            pltpu.VMEM((1, chans), jnp.float32),
            pltpu.VMEM((l2, chans), jnp.bfloat16),
            pltpu.VMEM((1, l2), jnp.float32),
            pltpu.VMEM((1, rows), jnp.int32),
            pltpu.VMEM((1, rows), jnp.int32),
            pltpu.VMEM((fdev + 2, hdev + 2, width, chans), jnp.bfloat16),
            pltpu.VMEM((3, 3, chans, 3 * chans), jnp.bfloat16),
            pltpu.VMEM((held * pitch, chans), jnp.float32),
            pltpu.VMEM((chans // l2 * chans, chans), jnp.bfloat16),
            pltpu.VMEM((n_tm * slots_per, held), jnp.bfloat16),
            pltpu.VMEM((2, 8, chans), jnp.float32),
            pltpu.VMEM((n, 8, chans), jnp.float32),
            pltpu.VMEM((n_tm, sent, lat), jnp.bfloat16),
            pltpu.SemaphoreType.DMA((10,)),
            pltpu.SemaphoreType.DMA((13,)),
            pltpu.SemaphoreType.DMA((13,)),
            pltpu.SemaphoreType.DMA((n,)),
            pltpu.SemaphoreType.DMA((n,)),
            pltpu.SemaphoreType.DMA((chunks, n_tm)),
            pltpu.SemaphoreType.DMA((chunks, n_tm)),
            pltpu.SemaphoreType.DMA,
        ],
        compiler_params=pltpu.CompilerParams(
            collective_id=0, has_side_effects=True, vmem_limit_bytes=VMEM - kept_bytes
        ),
    )(
        frame_counts.reshape(1, 1),
        video[0],
        conv_weight,
        norm_gain.reshape(1, chans),
        norm_shift.reshape(1, chans),
        quant_weight.T,
        quant_bias.reshape(1, l2),
        row_dest.reshape(1, rows),
    )
    merged = pl.pallas_call(
        functools.partial(merge, cap, capb),
        out_shape=jax.ShapeDtypeStruct((n_tm, cap, lat), jnp.bfloat16),
        in_specs=[pl.BlockSpec(memory_space=pltpu.VMEM)],
        out_specs=pl.BlockSpec(memory_space=pltpu.VMEM),
        compiler_params=pltpu.CompilerParams(vmem_limit_bytes=16 * 1024 * 1024),
    )(out)
    return merged.reshape(1, 1, 1, n_tm, cap, lat)


def solution(mesh):
    return jax.shard_map(
        functools.partial(body, mesh.shape["tm"], mesh.shape["space"]),
        mesh=mesh,
        in_specs=(
            P("clip", "tm", "space", None, None),
            P("clip"),
            P(),
            P(),
            P(),
            P(),
            P(),
            P("clip", "tm", "space", None, None),
        ),
        out_specs=P("clip", "tm", "space", None, None, None),
        check_vma=False,
    )
```

```python
import functools

import jax
import jax.numpy as jnp
from jax import lax
from jax.experimental import pallas as pl
from jax.experimental.pallas import tpu as pltpu
from jax.sharding import PartitionSpec as P

GROUPS = 32
MESH = pl.DeviceIdType.MESH
TILES = 8
VMEM = 64 * 1024 * 1024


def kernel(
    n_tm,
    n_space,
    cap,
    capb,
    own_slots,
    slots_per,
    pitch,
    count_hbm,
    video,
    weight,
    gain_hbm,
    shift_hbm,
    qw_hbm,
    qb_hbm,
    dest_hbm,
    out,
    count_ref,
    gain_ref,
    shift_ref,
    qw_ref,
    qb_ref,
    dest_ref,
    next_ref,
    xs,
    wb,
    act,
    wq,
    place,
    stats,
    gathered,
    bias_ref,
    outgoing,
    extra,
    extra_in,
    local_sem,
    halo_send,
    halo_recv,
    stat_send,
    stat_recv,
    row_send,
    row_recv,
    extra_send,
    extra_recv,
    token_sem,
):
    fdev, hdev, width, chans = video.shape
    l2 = qw_ref.shape[0]
    rows = fdev * hdev
    held = place.shape[1]
    folded = chans // l2
    lat = width * l2
    n = n_tm * n_space
    tm, space = lax.axis_index("tm"), lax.axis_index("space")
    me = tm * n_space + space
    first_tm, last_tm = tm == 0, tm == n_tm - 1

    def at(peer):
        return {"tm": peer // n_space, "space": lax.rem(peer, n_space)}

    barrier = pltpu.get_barrier_semaphore()

    near = n_tm == 2
    later = {"tm": lax.rem(tm + 1, n_tm)}
    earlier = {"tm": lax.rem(tm + n_tm - 1, n_tm)}
    above = {"space": lax.rem(space + n_space - 1, n_space)}
    below = {"space": lax.rem(space + 1, n_space)}

    def tell(sem, device):
        pl.semaphore_signal(sem, inc=1, device_id=device, device_id_type=MESH)

    if near:
        tell(barrier, later)

        @pl.when(space > 0)
        def _():
            tell(barrier, above)

        @pl.when(space < n_space - 1)
        def _():
            tell(barrier, below)

    else:

        @pl.loop(1, n)
        def _(step):
            tell(barrier, at(lax.rem(me + step, n)))

    own = pltpu.make_async_copy(
        video, xs.at[pl.ds(1, fdev), pl.ds(1, hdev)], local_sem.at[0]
    )
    own.start()
    taps = [
        pltpu.make_async_copy(
            weight.at[:, :, dw],
            wb.at[:, :, :, pl.ds(dw * chans, chans)],
            local_sem.at[1 + dw],
        )
        for dw in range(3)
    ]
    for tap in taps:
        tap.start()

    smalls = [
        pltpu.make_async_copy(src, dst, local_sem.at[4 + i])
        for i, (src, dst) in enumerate(
            [
                (qw_hbm, qw_ref),
                (qb_hbm, qb_ref),
                (dest_hbm, dest_ref),
                (gain_hbm, gain_ref),
                (shift_hbm, shift_ref),
                (count_hbm, count_ref),
            ]
        )
    ]
    for small in smalls:
        small.start()

    def prepare():
        zero_row = jnp.zeros((fdev + 2, width, chans), jnp.bfloat16)

        @pl.when(space == 0)
        def _():
            xs[:, 0] = zero_row

        @pl.when(space == n_space - 1)
        def _():
            xs[:, hdev + 1] = zero_row

        zero_frame = jnp.zeros((hdev * pitch, chans), jnp.float32)

        @pl.when(tm > 0)
        def _():
            act[pl.ds(0, hdev * pitch), :] = zero_frame

        @pl.when(tm == n_tm - 1)
        def _():
            act[pl.ds(rows * pitch, hdev * pitch), :] = zero_frame

        spare = held - rows - hdev
        act[pl.ds((rows + hdev) * pitch, spare * pitch), :] = jnp.zeros(
            (spare * pitch, chans), jnp.float32
        )

        for small in smalls:
            small.wait()
        lane = lax.broadcasted_iota(jnp.int32, (l2, chans), 1)
        sub = lax.broadcasted_iota(jnp.int32, (l2, chans), 0)
        spread = jnp.zeros((l2, chans), jnp.float32)
        for i in range(folded):
            pick = jnp.where(lane == sub + i * l2, 1.0, 0.0)
            spread = spread + pick
            wq[pl.ds(i * chans, chans), :] = lax.dot_general(
                qw_ref[...],
                pick.astype(jnp.bfloat16),
                (((0,), (0,)), ((), ())),
                preferred_element_type=jnp.float32,
            ).astype(jnp.bfloat16)
        bias_ref[...] = jnp.dot(
            qb_ref[...],
            spread,
            precision=lax.Precision.HIGHEST,
            preferred_element_type=jnp.float32,
        )
        stats[...] = jnp.zeros_like(stats)

    @pl.when(tm == 0)
    def _():
        prepare()

    if near:
        outer = (space == 0) | (space == n_space - 1)

        @pl.when(outer)
        def _():
            pl.semaphore_wait(barrier, min(n_space, 2))

        @pl.when(~outer)
        def _():
            pl.semaphore_wait(barrier, 3)

    else:
        pl.semaphore_wait(barrier, n - 1)

    def token(hop):
        if not near:
            return

        @pl.when(space == hop)
        def _():
            if hop > 0:
                pl.semaphore_wait(token_sem.at[0], 1)
            if hop < n_space - 1:
                tell(token_sem.at[0], below)

        @pl.when(space == n_space - 1 - hop)
        def _():
            if hop > 0:
                pl.semaphore_wait(token_sem.at[1], 1)
            if hop < n_space - 1:
                tell(token_sem.at[1], above)

    def remote(src, dst, index, device):
        return pltpu.make_async_remote_copy(
            src_ref=src,
            dst_ref=dst,
            send_sem=halo_send.at[index],
            recv_sem=halo_recv.at[index],
            device_id=device,
            device_id_type=MESH,
        )

    after = fdev + 1

    def frame_copies(source, target, index, device):
        return [
            remote(video.at[source, 0], xs.at[target, 1], index, device),
            remote(video.at[source, hdev - 1], xs.at[target, hdev], index + 1, device),
            remote(
                video.at[source, pl.ds(1, hdev - 2)],
                xs.at[target, pl.ds(2, hdev - 2)],
                index + 2,
                device,
            ),
        ]

    def corner_copies(target, index):
        return [
            remote(xs.at[target, 1], xs.at[target, hdev + 1], index, above),
            remote(xs.at[target, hdev], xs.at[target, 0], index + 1, below),
        ]

    forward = frame_copies(fdev - 1, 0, 0, later)
    back = frame_copies(0, after, 3, earlier)
    forward_corners = corner_copies(0, 6)
    back_corners = corner_copies(after, 8)
    up = remote(video.at[:, 0], xs.at[pl.ds(1, fdev), hdev + 1], 10, above)
    down = remote(video.at[:, hdev - 1], xs.at[pl.ds(1, fdev), 0], 11, below)
    dest_copy = remote(dest_hbm, next_ref, 12, earlier)

    @pl.when(tm < n_tm - 1)
    def _():
        for copy in forward:
            copy.start()

    @pl.when(tm > 0)
    def _():
        for copy in back:
            copy.start()

    @pl.when(space > 0)
    def _():
        up.start()

    @pl.when(space < n_space - 1)
    def _():
        down.start()

    @pl.when(tm > 0)
    def _():
        dest_copy.start()

    token(0)

    @pl.when(tm > 0)
    def _():
        prepare()

    count = count_ref[...]

    def valid(frame):
        ids = jnp.full((1, chans), 0, jnp.int32) + (tm * fdev + frame)
        return jnp.where(ids < count, 1.0, 0.0)

    cell = lax.broadcasted_iota(jnp.int32, (width, chans), 0)

    def accumulate(fs, taps_of, fresh, final, hs):
        items = [(f, h) for f in fs for h in hs]
        m = len(items) * width

        def index(f, dt):
            p = f - 1 + dt
            return 1 if f == 0 or (p == 0 and len(fs) == fdev) else p

        pieces = [
            jnp.concatenate([xs[index(f, dt), h + dh] for f, h in items], axis=0)
            for dt in taps_of
            for dh in range(3)
        ]
        kernel_part = wb[pl.ds(taps_of[0], len(taps_of))].reshape(-1, 3 * chans)
        y = jnp.dot(
            jnp.concatenate(pieces, axis=1), kernel_part, preferred_element_type=jnp.float32
        )
        for i, (f, h) in enumerate(items):
            part = y[i * width : (i + 1) * width]
            before = pltpu.roll(part[:, :chans], 1, 0)
            after_ = pltpu.roll(part[:, 2 * chans :], width - 1, 0)
            total = (
                part[:, chans : 2 * chans]
                + jnp.where(cell == 0, 0.0, before)
                + jnp.where(cell == width - 1, 0.0, after_)
            )
            spot = pl.ds((f * hdev + h) * pitch, width)
            if not fresh:
                total = total + act[spot, :]
            if final:
                total = total * valid(f)
                stats[0] += jnp.sum(total.reshape(width // 8, 8, chans), axis=0)
                stats[1] += jnp.sum((total * total).reshape(width // 8, 8, chans), axis=0)
            act[spot, :] = total

    inner, edge = list(range(1, hdev - 1)), [0, hdev - 1]

    own.wait()
    for tap in taps:
        tap.wait()

    def own_taps(part):
        @pl.when(tm == 0)
        def _():
            accumulate(range(fdev), (0, 1, 2), True, True, part)

        @pl.when(tm > 0)
        def _():
            accumulate(range(2, fdev), (0, 1, 2), True, True, part)
            accumulate([1], (1, 2), True, False, part)

        @pl.when(tm < n_tm - 1)
        def _():
            accumulate([fdev], (0, 1), True, False, part)

    own_taps(inner)
    if n_space > 2:
        token(1)

    def pass_corners(arrived, corners):
        arrived[0].wait_recv()
        arrived[1].wait_recv()

        @pl.when(space > 0)
        def _():
            corners[0].start()

        @pl.when(space < n_space - 1)
        def _():
            corners[1].start()

    @pl.when(tm > 0)
    def _():
        pass_corners(forward, forward_corners)

    @pl.when(tm < n_tm - 1)
    def _():
        pass_corners(back, back_corners)

    @pl.when(space < n_space - 1)
    def _():
        up.wait_recv()

    @pl.when(space > 0)
    def _():
        down.wait_recv()

    own_taps(edge)
    for hop in range(2, n_space - 1):
        token(hop)

    def corners_in(corners):
        @pl.when(space < n_space - 1)
        def _():
            corners[0].wait_recv()

        @pl.when(space > 0)
        def _():
            corners[1].wait_recv()

    @pl.when(tm > 0)
    def _():
        corners_in(forward_corners)
        forward[2].wait_recv()
        accumulate([1], (0,), False, True, range(hdev))

    @pl.when(tm < n_tm - 1)
    def _():
        corners_in(back_corners)
        back[2].wait_recv()
        accumulate([fdev], (2,), False, True, range(hdev))

    halves = [jnp.sum(stats[i], axis=0, keepdims=True) for i in range(2)]
    line = lax.broadcasted_iota(jnp.int32, (8, chans), 0)
    gathered[me] = jnp.where(line == 0, halves[0], jnp.where(line == 1, halves[1], 0.0))

    def stat_copy(step):
        return pltpu.make_async_remote_copy(
            src_ref=gathered.at[me],
            dst_ref=gathered.at[me],
            send_sem=stat_send.at[step],
            recv_sem=stat_recv.at[me],
            device_id=at(lax.rem(me + step, n)),
            device_id_type=MESH,
        )

    def stat_arrival(step):
        sender = lax.rem(me + step, n)
        return pltpu.make_async_remote_copy(
            src_ref=gathered.at[sender],
            dst_ref=gathered.at[sender],
            send_sem=stat_send.at[step],
            recv_sem=stat_recv.at[sender],
            device_id=at(sender),
            device_id_type=MESH,
        )

    if n_space > 1:
        token(n_space - 1)

    @pl.loop(1, n)
    def _(step):
        stat_copy(step).start()

    @pl.when(tm < n_tm - 1)
    def _():
        dest_copy.wait_recv()

    @pl.when(tm == n_tm - 1)
    def _():
        next_ref[...] = jnp.zeros_like(next_ref)

    def numbers(shape, axis):
        return lax.broadcasted_iota(jnp.int32, shape, axis)

    along, across = numbers((held, held), 0), numbers((held, held), 1)
    source, column = numbers((rows, held), 0), numbers((rows, held), 1)
    named = jnp.dot(
        dest_ref[...].astype(jnp.float32),
        jnp.where(source == column, 1.0, 0.0),
        precision=lax.Precision.HIGHEST,
        preferred_element_type=jnp.float32,
    ) + jnp.dot(
        next_ref[...].astype(jnp.float32),
        jnp.where((source + rows == column) & (source < hdev), 1.0, 0.0),
        precision=lax.Precision.HIGHEST,
        preferred_element_type=jnp.float32,
    )
    wide_named = jnp.broadcast_to(named, (held, held))
    tall_named = jnp.sum(jnp.where(across == along, wide_named, 0.0), axis=1, keepdims=True)
    alike = (tall_named == wide_named) & (along < across) & ((along < rows) == (across < rows))
    rank = jnp.sum(jnp.where(alike, 1.0, 0.0), axis=0, keepdims=True)
    position = numbers((1, held), 1)
    here = (
        ((position < hdev) & first_tm)
        | ((position >= hdev) & (position < rows))
        | ((position >= rows) & (position < rows + hdev) & (~last_tm))
    )
    slot = named * slots_per + rank + jnp.where(position >= rows, 1.0 * own_slots, 0.0)
    slot = jnp.where(here, slot, -1.0)
    slots = numbers((place.shape[0], held), 0).astype(jnp.float32)
    place[...] = jnp.where(slots == slot, 1.0, 0.0).astype(jnp.bfloat16)

    @pl.loop(1, n)
    def _(step):
        stat_arrival(step).wait_recv()

    sums = jnp.sum(gathered[...], axis=0)
    position = lax.broadcasted_iota(jnp.int32, (8, chans), 1)
    per = chans // GROUPS
    reach = 1
    while reach < per:
        low = lax.rem(position // reach, 2) == 0
        sums = sums + jnp.where(
            low, pltpu.roll(sums, chans - reach, 1), pltpu.roll(sums, reach, 1)
        )
        reach *= 2
    amount = jnp.full((1, chans), 1, jnp.int32) * count
    total_count = amount.astype(jnp.float32) * (n_space * hdev * width * per)
    mean = sums[0:1] / total_count
    var = jnp.maximum(sums[1:2] / total_count - mean * mean, 0.0)
    scale = lax.rsqrt(var + 1e-06) * gain_ref[...]
    offset = shift_ref[...] - mean * scale
    scale, offset = 0.5 * scale, 0.5 * offset
    row = numbers((held, chans), 0)
    frame = jnp.zeros((held, chans), jnp.int32) + tm * fdev
    for f in range(1, fdev + 1):
        frame = frame + jnp.where(row >= f * hdev, 1, 0)
    frame_masks = jnp.where(frame < count, 1.0, 0.0)
    chunks = lat // (TILES * chans)

    wide_cells = TILES * chans

    def columns(chunk):
        return pl.ds(pl.multiple_of(chunk * wide_cells, wide_cells), wide_cells)

    def row_copies(chunk, step, sender):
        peer = lax.rem(tm + step, n_tm)
        place_of = peer if sender else tm
        return [
            pltpu.make_async_remote_copy(
                src_ref=source.at[peer, :, columns(chunk)],
                dst_ref=target.at[place_of, :, columns(chunk)],
                send_sem=send.at[chunk, step],
                recv_sem=recv.at[chunk, place_of],
                device_id={"tm": peer},
                device_id_type=MESH,
            )
            for source, target, send, recv in [
                (outgoing, out, row_send, row_recv),
                (extra, extra_in, extra_send, extra_recv),
            ]
        ]

    @pl.loop(0, chunks)
    def _(chunk):
        hidden = []
        for j in range(TILES):
            cells = []
            for i in range(folded):
                w = (chunk * TILES + j) * folded + i
                half = act[pl.ds(w, held, stride=pitch), :] * scale + offset
                cells.append((half + half * jnp.tanh(half)) * frame_masks)
            hidden.append(jnp.concatenate(cells, axis=1))
        hidden = jnp.concatenate(hidden, axis=0).astype(jnp.bfloat16)
        moments = (
            jnp.dot(hidden, wq[...], preferred_element_type=jnp.float32) + bias_ref[...]
        )
        wide = jnp.concatenate(
            [moments[j * held : (j + 1) * held] for j in range(TILES)], axis=1
        ).astype(jnp.bfloat16)
        routed = jnp.dot(place[...], wide, preferred_element_type=jnp.float32)
        for d in range(n_tm):
            start = d * slots_per
            outgoing[d, :, columns(chunk)] = routed[start : start + cap].astype(jnp.bfloat16)
            start = start + own_slots
            extra[d, :, columns(chunk)] = routed[start : start + capb].astype(jnp.bfloat16)

        @pl.loop(1, n_tm)
        def _(step):
            own, more = row_copies(chunk, step, False)
            own.start()

            @pl.when(tm < n_tm - 1)
            def _():
                more.start()

        mine = jnp.dot(
            place[pl.ds(pl.multiple_of(tm * slots_per, slots_per), slots_per), :],
            wide,
            preferred_element_type=jnp.float32,
        )
        out[tm, :, columns(chunk)] = mine[:cap].astype(jnp.bfloat16)
        extra_in[tm, :, columns(chunk)] = mine[own_slots : own_slots + capb].astype(
            jnp.bfloat16
        )

    @pl.loop(1, n)
    def _(step):
        stat_copy(step).wait_send()

    def sent(corners):
        @pl.when(space > 0)
        def _():
            corners[0].wait_send()

        @pl.when(space < n_space - 1)
        def _():
            corners[1].wait_send()

    @pl.when(tm < n_tm - 1)
    def _():
        for copy in forward:
            copy.wait_send()
        sent(back_corners)

    @pl.when(tm > 0)
    def _():
        for copy in back:
            copy.wait_send()
        dest_copy.wait_send()
        sent(forward_corners)

    @pl.when(space > 0)
    def _():
        up.wait_send()

    @pl.when(space < n_space - 1)
    def _():
        down.wait_send()

    @pl.loop(0, chunks)
    def _(chunk):
        @pl.loop(1, n_tm)
        def _(step):
            own, more = row_copies(chunk, step, False)
            own.wait_send()

            @pl.when(tm < n_tm - 1)
            def _():
                more.wait_send()

            own, more = row_copies(chunk, step, True)
            own.wait_recv()

            @pl.when(lax.rem(tm + step, n_tm) < n_tm - 1)
            def _():
                more.wait_recv()

        @pl.loop(1, n_tm)
        def _(t):
            out[t, :capb, columns(chunk)] = (
                out[t, :capb, columns(chunk)].astype(jnp.float32)
                + extra_in[t - 1, :, columns(chunk)].astype(jnp.float32)
            ).astype(jnp.bfloat16)


def hand_over(source, target, sem):
    copy = pltpu.make_async_copy(source, target, sem)
    copy.start()
    copy.wait()


def body(
    n_tm,
    n_space,
    video,
    frame_counts,
    conv_weight,
    norm_gain,
    norm_shift,
    quant_weight,
    quant_bias,
    row_dest,
):
    clips, fdev, hdev, width, chans = video.shape
    l2 = quant_weight.shape[1]
    rows = fdev * hdev
    lat = width * l2
    cap = min(max(2, 2 * rows // n_tm), rows)
    capb = min(cap, hdev)
    own_slots = -(-cap // 8) * 8
    slots_per = own_slots + -(-capb // 8) * 8
    held = -(-(rows + hdev) // 16) * 16
    pitch = width + 8
    n = n_tm * n_space
    chunks = lat // (TILES * chans)
    kept_bytes = n_tm * own_slots * lat * 2 + 128 * 1024
    hbm = pl.BlockSpec(memory_space=pltpu.HBM)
    out = pl.pallas_call(
        functools.partial(kernel, n_tm, n_space, cap, capb, own_slots, slots_per, pitch),
        out_shape=pltpu.VMEM((n_tm, cap, lat), jnp.bfloat16),
        in_specs=[hbm] * 8,
        out_specs=pl.BlockSpec(memory_space=pltpu.VMEM),
        scratch_shapes=[
            pltpu.VMEM((1, 1), jnp.int32),
            pltpu.VMEM((1, chans), jnp.float32),
            pltpu.VMEM((1, chans), jnp.float32),
            pltpu.VMEM((l2, chans), jnp.bfloat16),
            pltpu.VMEM((1, l2), jnp.float32),
            pltpu.VMEM((1, rows), jnp.int32),
            pltpu.VMEM((1, rows), jnp.int32),
            pltpu.VMEM((fdev + 2, hdev + 2, width, chans), jnp.bfloat16),
            pltpu.VMEM((3, 3, chans, 3 * chans), jnp.bfloat16),
            pltpu.VMEM((held * pitch, chans), jnp.float32),
            pltpu.VMEM((chans // l2 * chans, chans), jnp.bfloat16),
            pltpu.VMEM((n_tm * slots_per, held), jnp.bfloat16),
            pltpu.VMEM((2, 8, chans), jnp.float32),
            pltpu.VMEM((n, 8, chans), jnp.float32),
            pltpu.VMEM((1, chans), jnp.float32),
            pltpu.VMEM((n_tm, cap, lat), jnp.bfloat16),
            pltpu.VMEM((n_tm, capb, lat), jnp.bfloat16),
            pltpu.VMEM((n_tm, capb, lat), jnp.bfloat16),
            pltpu.SemaphoreType.DMA((10,)),
            pltpu.SemaphoreType.DMA((13,)),
            pltpu.SemaphoreType.DMA((13,)),
            pltpu.SemaphoreType.DMA((n,)),
            pltpu.SemaphoreType.DMA((n,)),
            *[pltpu.SemaphoreType.DMA((chunks, n_tm))] * 4,
            pltpu.SemaphoreType.REGULAR((2,)),
        ],
        compiler_params=pltpu.CompilerParams(
            collective_id=0, has_side_effects=True, vmem_limit_bytes=VMEM - kept_bytes
        ),
    )(
        frame_counts.reshape(1, 1),
        video[0],
        conv_weight,
        norm_gain.reshape(1, chans),
        norm_shift.reshape(1, chans),
        quant_weight.T,
        quant_bias.reshape(1, l2),
        row_dest.reshape(1, rows),
    )
    return out.reshape(1, 1, 1, n_tm, cap, lat)


def solution(mesh):
    return jax.shard_map(
        functools.partial(body, mesh.shape["tm"], mesh.shape["space"]),
        mesh=mesh,
        in_specs=(
            P("clip", "tm", "space", None, None),
            P("clip"),
            P(),
            P(),
            P(),
            P(),
            P(),
            P("clip", "tm", "space", None, None),
        ),
        out_specs=P("clip", "tm", "space", None, None, None),
        check_vma=False,
    )
```

```python
import functools

import jax
import jax.numpy as jnp
from jax import lax
from jax.experimental import pallas as pl
from jax.experimental.pallas import tpu as pltpu
from jax.sharding import PartitionSpec as P

GROUPS = 32
MESH = pl.DeviceIdType.MESH
TILES = 8
VMEM = 64 * 1024 * 1024


def kernel(
    n_tm,
    n_space,
    cap,
    capb,
    own_slots,
    slots_per,
    pitch,
    count_hbm,
    video,
    weight,
    gain_hbm,
    shift_hbm,
    qw_hbm,
    qb_hbm,
    dest_hbm,
    out,
    count_ref,
    gain_ref,
    shift_ref,
    qw_ref,
    qb_ref,
    dest_ref,
    next_ref,
    xs,
    wb,
    folded_taps,
    act,
    wq,
    place,
    stats,
    gathered,
    bias_ref,
    outgoing,
    extra,
    extra_in,
    local_sem,
    halo_send,
    halo_recv,
    stat_send,
    stat_recv,
    row_send,
    row_recv,
    extra_send,
    extra_recv,
    token_sem,
):
    fdev, hdev, width, chans = video.shape
    l2 = qw_ref.shape[0]
    rows = fdev * hdev
    held = place.shape[1]
    folded = chans // l2
    lat = width * l2
    n = n_tm * n_space
    tm, space = lax.axis_index("tm"), lax.axis_index("space")
    me = tm * n_space + space
    first_tm, last_tm = tm == 0, tm == n_tm - 1

    def at(peer):
        return {"tm": peer // n_space, "space": lax.rem(peer, n_space)}

    barrier = pltpu.get_barrier_semaphore()

    near = n_tm == 2
    later = {"tm": lax.rem(tm + 1, n_tm)}
    earlier = {"tm": lax.rem(tm + n_tm - 1, n_tm)}
    above = {"space": lax.rem(space + n_space - 1, n_space)}
    below = {"space": lax.rem(space + 1, n_space)}

    def tell(sem, device):
        pl.semaphore_signal(sem, inc=1, device_id=device, device_id_type=MESH)

    if near:
        tell(barrier, later)

        @pl.when(space > 0)
        def _():
            tell(barrier, above)

        @pl.when(space < n_space - 1)
        def _():
            tell(barrier, below)

    else:

        @pl.loop(1, n)
        def _(step):
            tell(barrier, at(lax.rem(me + step, n)))

    taps = [
        pltpu.make_async_copy(
            weight.at[:, :, dw],
            wb.at[:, :, :, pl.ds(dw * chans, chans)],
            local_sem.at[1 + dw],
        )
        for dw in range(3)
    ]
    for tap in taps:
        tap.start()
    own = pltpu.make_async_copy(
        video, xs.at[pl.ds(1, fdev), pl.ds(1, hdev)], local_sem.at[0]
    )
    own.start()

    smalls = [
        pltpu.make_async_copy(src, dst, local_sem.at[4 + i])
        for i, (src, dst) in enumerate(
            [
                (qw_hbm, qw_ref),
                (qb_hbm, qb_ref),
                (dest_hbm, dest_ref),
                (gain_hbm, gain_ref),
                (shift_hbm, shift_ref),
                (count_hbm, count_ref),
            ]
        )
    ]
    for small in smalls:
        small.start()

    def prepare():
        zero_row = jnp.zeros((fdev + 2, width, chans), jnp.bfloat16)

        @pl.when(space == 0)
        def _():
            xs[:, 0] = zero_row

        @pl.when(space == n_space - 1)
        def _():
            xs[:, hdev + 1] = zero_row

        zero_frame = jnp.zeros((hdev * pitch, chans), jnp.float32)

        @pl.when(tm > 0)
        def _():
            act[pl.ds(0, hdev * pitch), :] = zero_frame

        @pl.when(tm == n_tm - 1)
        def _():
            act[pl.ds(rows * pitch, hdev * pitch), :] = zero_frame

        spare = held - rows - hdev
        act[pl.ds((rows + hdev) * pitch, spare * pitch), :] = jnp.zeros(
            (spare * pitch, chans), jnp.float32
        )

        for small in smalls:
            small.wait()
        lane = lax.broadcasted_iota(jnp.int32, (l2, chans), 1)
        sub = lax.broadcasted_iota(jnp.int32, (l2, chans), 0)
        spread = jnp.zeros((l2, chans), jnp.float32)
        for i in range(folded):
            pick = jnp.where(lane == sub + i * l2, 1.0, 0.0)
            spread = spread + pick
            wq[pl.ds(i * chans, chans), :] = lax.dot_general(
                qw_ref[...],
                pick.astype(jnp.bfloat16),
                (((0,), (0,)), ((), ())),
                preferred_element_type=jnp.float32,
            ).astype(jnp.bfloat16)
        bias_ref[...] = jnp.dot(
            qb_ref[...],
            spread,
            precision=lax.Precision.HIGHEST,
            preferred_element_type=jnp.float32,
        )
        stats[...] = jnp.zeros_like(stats)

    @pl.when(tm == 0)
    def _():
        prepare()

    if near:
        outer = (space == 0) | (space == n_space - 1)

        @pl.when(outer)
        def _():
            pl.semaphore_wait(barrier, min(n_space, 2))

        @pl.when(~outer)
        def _():
            pl.semaphore_wait(barrier, 3)

    else:
        pl.semaphore_wait(barrier, n - 1)

    def token(hop):
        if not near:
            return

        @pl.when(space == hop)
        def _():
            if hop > 0:
                pl.semaphore_wait(token_sem.at[0], 1)
            if hop < n_space - 1:
                tell(token_sem.at[0], below)

        @pl.when(space == n_space - 1 - hop)
        def _():
            if hop > 0:
                pl.semaphore_wait(token_sem.at[1], 1)
            if hop < n_space - 1:
                tell(token_sem.at[1], above)

    def remote(src, dst, index, device):
        return pltpu.make_async_remote_copy(
            src_ref=src,
            dst_ref=dst,
            send_sem=halo_send.at[index],
            recv_sem=halo_recv.at[index],
            device_id=device,
            device_id_type=MESH,
        )

    after = fdev + 1

    def frame_copies(source, target, index, device):
        return [
            remote(video.at[source, 0], xs.at[target, 1], index, device),
            remote(video.at[source, hdev - 1], xs.at[target, hdev], index + 1, device),
            remote(
                video.at[source, pl.ds(1, hdev - 2)],
                xs.at[target, pl.ds(2, hdev - 2)],
                index + 2,
                device,
            ),
        ]

    def corner_copies(target, index):
        return [
            remote(xs.at[target, 1], xs.at[target, hdev + 1], index, above),
            remote(xs.at[target, hdev], xs.at[target, 0], index + 1, below),
        ]

    forward = frame_copies(fdev - 1, 0, 0, later)
    back = frame_copies(0, after, 3, earlier)
    forward_corners = corner_copies(0, 6)
    back_corners = corner_copies(after, 8)
    half = fdev // 2

    def row_halo(start, count, index):
        source, target = pl.ds(start, count), pl.ds(start + 1, count)
        return [
            remote(video.at[source, 0], xs.at[target, hdev + 1], index, above),
            remote(video.at[source, hdev - 1], xs.at[target, 0], index + 1, below),
        ]

    early_rows, late_rows = row_halo(0, half, 10), row_halo(half, fdev - half, 13)
    dest_copy = remote(dest_hbm, next_ref, 12, earlier)

    @pl.when(tm > 0)
    def _():
        for copy in back:
            copy.start()

    @pl.when(space > 0)
    def _():
        early_rows[0].start()
        late_rows[0].start()

    @pl.when(space < n_space - 1)
    def _():
        early_rows[1].start()
        late_rows[1].start()

    @pl.when(tm < n_tm - 1)
    def _():
        for copy in forward:
            copy.start()

    @pl.when(tm > 0)
    def _():
        dest_copy.start()

    token(0)

    @pl.when(tm > 0)
    def _():
        prepare()

    count = count_ref[...]

    def valid(frame):
        ids = jnp.full((1, chans), 0, jnp.int32) + (tm * fdev + frame)
        return jnp.where(ids < count, 1.0, 0.0)

    cell = lax.broadcasted_iota(jnp.int32, (width, chans), 0)

    def accumulate(fs, taps_of, fresh, final, hs):
        items = [(f, h) for f in fs for h in hs]
        m = len(items) * width

        def index(f, dt):
            p = f - 1 + dt
            return 1 if p == 0 and len(taps_of) == 3 else p

        if fs == [0]:
            frames_of = [[1], [1]]
            kernel_part = folded_taps[...].reshape(-1, 3 * chans)
        else:
            frames_of = [[index(f, dt) for f in fs] for dt in taps_of]
            kernel_part = wb[pl.ds(taps_of[0], len(taps_of))].reshape(-1, 3 * chans)
        pieces = [
            jnp.concatenate([xs[p, h + dh] for p in ps for h in hs], axis=0)
            for ps in frames_of
            for dh in range(3)
        ]
        y = jnp.dot(
            jnp.concatenate(pieces, axis=1), kernel_part, preferred_element_type=jnp.float32
        )
        for i, (f, h) in enumerate(items):
            part = y[i * width : (i + 1) * width]
            before = pltpu.roll(part[:, :chans], 1, 0)
            after_ = pltpu.roll(part[:, 2 * chans :], width - 1, 0)
            total = (
                part[:, chans : 2 * chans]
                + jnp.where(cell == 0, 0.0, before)
                + jnp.where(cell == width - 1, 0.0, after_)
            )
            spot = pl.ds((f * hdev + h) * pitch, width)
            if not fresh:
                total = total + act[spot, :]
            if final:
                total = total * valid(f)
                stats[0] += jnp.sum(total.reshape(width // 8, 8, chans), axis=0)
                stats[1] += jnp.sum((total * total).reshape(width // 8, 8, chans), axis=0)
            act[spot, :] = total

    inner, edge = list(range(1, hdev - 1)), [0, hdev - 1]

    @pl.when(tm == 0)
    def _():
        for tap in taps:
            tap.wait()

        @pl.loop(0, 3)
        def _(dh):
            total = sum(wb[dt, dh].astype(jnp.float32) for dt in range(3))
            high = total.astype(jnp.bfloat16)
            folded_taps[0, dh] = high
            folded_taps[1, dh] = (total - high.astype(jnp.float32)).astype(jnp.bfloat16)

    own.wait()

    @pl.when(tm > 0)
    def _():
        for tap in taps:
            tap.wait()

    def pass_corners(arrived, corners):
        arrived[0].wait_recv()
        arrived[1].wait_recv()

        @pl.when(space > 0)
        def _():
            corners[0].start()

        @pl.when(space < n_space - 1)
        def _():
            corners[1].start()

    @pl.when(tm == 0)
    def _():
        accumulate(range(1, fdev), (0, 1, 2), True, True, inner)
        accumulate([0], (0, 1, 2), True, True, inner)

    @pl.when(tm > 0)
    def _():
        accumulate(range(2, fdev), (0, 1, 2), True, True, inner)
        pass_corners(forward, forward_corners)
        accumulate([1], (1, 2), True, False, inner)

    @pl.when(tm < n_tm - 1)
    def _():
        pass_corners(back, back_corners)
        accumulate([fdev], (0, 1), True, False, inner)

    if n_space > 2:
        token(1)

    def rows_in(copies):
        @pl.when(space < n_space - 1)
        def _():
            copies[0].wait_recv()

        @pl.when(space > 0)
        def _():
            copies[1].wait_recv()

    rows_in(early_rows)

    @pl.when(tm == 0)
    def _():
        accumulate(range(1, half), (0, 1, 2), True, True, edge)
        accumulate([0], (0, 1, 2), True, True, edge)

    rows_in(late_rows)

    @pl.when(tm == 0)
    def _():
        accumulate(range(half, fdev), (0, 1, 2), True, True, edge)

    @pl.when(tm > 0)
    def _():
        accumulate(range(2, fdev), (0, 1, 2), True, True, edge)
        accumulate([1], (1, 2), True, False, edge)

    @pl.when(tm < n_tm - 1)
    def _():
        accumulate([fdev], (0, 1), True, False, edge)

    for hop in range(2, n_space - 1):
        token(hop)

    def corners_in(corners):
        @pl.when(space < n_space - 1)
        def _():
            corners[0].wait_recv()

        @pl.when(space > 0)
        def _():
            corners[1].wait_recv()

    @pl.when(tm > 0)
    def _():
        corners_in(forward_corners)
        forward[2].wait_recv()
        accumulate([1], (0,), False, True, range(hdev))

    @pl.when(tm < n_tm - 1)
    def _():
        back[2].wait_recv()
        accumulate([fdev], (2,), False, True, inner)
        corners_in(back_corners)
        accumulate([fdev], (2,), False, True, edge)

    halves = [jnp.sum(stats[i], axis=0, keepdims=True) for i in range(2)]
    line = lax.broadcasted_iota(jnp.int32, (8, chans), 0)
    gathered[me] = jnp.where(line == 0, halves[0], jnp.where(line == 1, halves[1], 0.0))

    def stat_copy(step):
        return pltpu.make_async_remote_copy(
            src_ref=gathered.at[me],
            dst_ref=gathered.at[me],
            send_sem=stat_send.at[step],
            recv_sem=stat_recv.at[me],
            device_id=at(lax.rem(me + step, n)),
            device_id_type=MESH,
        )

    def stat_arrival(step):
        sender = lax.rem(me + step, n)
        return pltpu.make_async_remote_copy(
            src_ref=gathered.at[sender],
            dst_ref=gathered.at[sender],
            send_sem=stat_send.at[step],
            recv_sem=stat_recv.at[sender],
            device_id=at(sender),
            device_id_type=MESH,
        )

    if n_space > 1:
        token(n_space - 1)

    @pl.loop(1, n)
    def _(step):
        stat_copy(step).start()

    @pl.when(tm < n_tm - 1)
    def _():
        dest_copy.wait_recv()

    @pl.when(tm == n_tm - 1)
    def _():
        next_ref[...] = jnp.zeros_like(next_ref)

    def numbers(shape, axis):
        return lax.broadcasted_iota(jnp.int32, shape, axis)

    along, across = numbers((held, held), 0), numbers((held, held), 1)
    source, column = numbers((rows, held), 0), numbers((rows, held), 1)
    named = jnp.dot(
        dest_ref[...].astype(jnp.float32),
        jnp.where(source == column, 1.0, 0.0),
        precision=lax.Precision.HIGHEST,
        preferred_element_type=jnp.float32,
    ) + jnp.dot(
        next_ref[...].astype(jnp.float32),
        jnp.where((source + rows == column) & (source < hdev), 1.0, 0.0),
        precision=lax.Precision.HIGHEST,
        preferred_element_type=jnp.float32,
    )
    wide_named = jnp.broadcast_to(named, (held, held))
    tall_named = jnp.sum(jnp.where(across == along, wide_named, 0.0), axis=1, keepdims=True)
    alike = (tall_named == wide_named) & (along < across) & ((along < rows) == (across < rows))
    rank = jnp.sum(jnp.where(alike, 1.0, 0.0), axis=0, keepdims=True)
    position = numbers((1, held), 1)
    here = (
        ((position < hdev) & first_tm)
        | ((position >= hdev) & (position < rows))
        | ((position >= rows) & (position < rows + hdev) & (~last_tm))
    )
    slot = named * slots_per + rank + jnp.where(position >= rows, 1.0 * own_slots, 0.0)
    slot = jnp.where(here, slot, -1.0)
    slots = numbers((place.shape[0], held), 0).astype(jnp.float32)
    place[...] = jnp.where(slots == slot, 1.0, 0.0).astype(jnp.bfloat16)

    @pl.loop(1, n)
    def _(step):
        stat_arrival(step).wait_recv()

    sums = jnp.sum(gathered[...], axis=0)
    position = lax.broadcasted_iota(jnp.int32, (8, chans), 1)
    per = chans // GROUPS
    reach = 1
    while reach < per:
        low = lax.rem(position // reach, 2) == 0
        sums = sums + jnp.where(
            low, pltpu.roll(sums, chans - reach, 1), pltpu.roll(sums, reach, 1)
        )
        reach *= 2
    amount = jnp.full((1, chans), 1, jnp.int32) * count
    total_count = amount.astype(jnp.float32) * (n_space * hdev * width * per)
    mean = sums[0:1] / total_count
    var = jnp.maximum(sums[1:2] / total_count - mean * mean, 0.0)
    scale = lax.rsqrt(var + 1e-06) * gain_ref[...]
    offset = shift_ref[...] - mean * scale
    scale, offset = 0.5 * scale, 0.5 * offset
    row = numbers((held, chans), 0)
    frame = jnp.zeros((held, chans), jnp.int32) + tm * fdev
    for f in range(1, fdev + 1):
        frame = frame + jnp.where(row >= f * hdev, 1, 0)
    frame_masks = jnp.where(frame < count, 1.0, 0.0)
    chunks = lat // (TILES * chans)

    wide_cells = TILES * chans

    def columns(chunk):
        return pl.ds(pl.multiple_of(chunk * wide_cells, wide_cells), wide_cells)

    def row_copies(chunk, step, sender):
        peer = lax.rem(tm + step, n_tm)
        place_of = peer if sender else tm
        return [
            pltpu.make_async_remote_copy(
                src_ref=source.at[peer, :, columns(chunk)],
                dst_ref=target.at[place_of, :, columns(chunk)],
                send_sem=send.at[chunk, step],
                recv_sem=recv.at[chunk, place_of],
                device_id={"tm": peer},
                device_id_type=MESH,
            )
            for source, target, send, recv in [
                (outgoing, out, row_send, row_recv),
                (extra, extra_in, extra_send, extra_recv),
            ]
        ]

    @functools.partial(lax.fori_loop, 0, chunks, init_val=None, unroll=True)
    def _(chunk, _carry):
        hidden = []
        for j in range(TILES):
            cells = []
            for i in range(folded):
                w = (chunk * TILES + j) * folded + i
                half = act[pl.ds(w, held, stride=pitch), :] * scale + offset
                cells.append((half + half * jnp.tanh(half)) * frame_masks)
            hidden.append(jnp.concatenate(cells, axis=1))
        hidden = jnp.concatenate(hidden, axis=0).astype(jnp.bfloat16)
        moments = (
            jnp.dot(hidden, wq[...], preferred_element_type=jnp.float32) + bias_ref[...]
        )
        wide = jnp.concatenate(
            [moments[j * held : (j + 1) * held] for j in range(TILES)], axis=1
        ).astype(jnp.bfloat16)
        routed = jnp.dot(place[...], wide, preferred_element_type=jnp.float32)
        for d in range(n_tm):
            start = d * slots_per
            outgoing[d, :, columns(chunk)] = routed[start : start + cap].astype(jnp.bfloat16)
            start = start + own_slots
            extra[d, :, columns(chunk)] = routed[start : start + capb].astype(jnp.bfloat16)

        @pl.loop(1, n_tm)
        def _(step):
            own, more = row_copies(chunk, step, False)
            own.start()

            @pl.when(tm < n_tm - 1)
            def _():
                more.start()

        mine = jnp.dot(
            place[pl.ds(pl.multiple_of(tm * slots_per, slots_per), slots_per), :],
            wide,
            preferred_element_type=jnp.float32,
        )
        out[tm, :, columns(chunk)] = mine[:cap].astype(jnp.bfloat16)
        extra_in[tm, :, columns(chunk)] = mine[own_slots : own_slots + capb].astype(
            jnp.bfloat16
        )

    @pl.loop(1, n)
    def _(step):
        stat_copy(step).wait_send()

    def sent(corners):
        @pl.when(space > 0)
        def _():
            corners[0].wait_send()

        @pl.when(space < n_space - 1)
        def _():
            corners[1].wait_send()

    @pl.when(tm < n_tm - 1)
    def _():
        for copy in forward:
            copy.wait_send()
        sent(back_corners)

    @pl.when(tm > 0)
    def _():
        for copy in back:
            copy.wait_send()
        dest_copy.wait_send()
        sent(forward_corners)

    @pl.when(space > 0)
    def _():
        early_rows[0].wait_send()
        late_rows[0].wait_send()

    @pl.when(space < n_space - 1)
    def _():
        early_rows[1].wait_send()
        late_rows[1].wait_send()

    @pl.loop(0, chunks)
    def _(chunk):
        @pl.loop(1, n_tm)
        def _(step):
            own, more = row_copies(chunk, step, False)
            own.wait_send()

            @pl.when(tm < n_tm - 1)
            def _():
                more.wait_send()

            own, more = row_copies(chunk, step, True)
            own.wait_recv()

            @pl.when(lax.rem(tm + step, n_tm) < n_tm - 1)
            def _():
                more.wait_recv()

        @pl.loop(1, n_tm)
        def _(t):
            out[t, :capb, columns(chunk)] = (
                out[t, :capb, columns(chunk)].astype(jnp.float32)
                + extra_in[t - 1, :, columns(chunk)].astype(jnp.float32)
            ).astype(jnp.bfloat16)


def hand_over(source, target, sem):
    copy = pltpu.make_async_copy(source, target, sem)
    copy.start()
    copy.wait()


def body(
    n_tm,
    n_space,
    video,
    frame_counts,
    conv_weight,
    norm_gain,
    norm_shift,
    quant_weight,
    quant_bias,
    row_dest,
):
    clips, fdev, hdev, width, chans = video.shape
    l2 = quant_weight.shape[1]
    rows = fdev * hdev
    lat = width * l2
    cap = min(max(2, 2 * rows // n_tm), rows)
    capb = min(cap, hdev)
    own_slots = -(-cap // 8) * 8
    slots_per = own_slots + -(-capb // 8) * 8
    held = -(-(rows + hdev) // 16) * 16
    pitch = width + 8
    n = n_tm * n_space
    chunks = lat // (TILES * chans)
    kept_bytes = n_tm * own_slots * lat * 2 + 128 * 1024
    hbm = pl.BlockSpec(memory_space=pltpu.HBM)
    out = pl.pallas_call(
        functools.partial(kernel, n_tm, n_space, cap, capb, own_slots, slots_per, pitch),
        out_shape=pltpu.VMEM((n_tm, cap, lat), jnp.bfloat16),
        in_specs=[hbm] * 8,
        out_specs=pl.BlockSpec(memory_space=pltpu.VMEM),
        scratch_shapes=[
            pltpu.VMEM((1, 1), jnp.int32),
            pltpu.VMEM((1, chans), jnp.float32),
            pltpu.VMEM((1, chans), jnp.float32),
            pltpu.VMEM((l2, chans), jnp.bfloat16),
            pltpu.VMEM((1, l2), jnp.float32),
            pltpu.VMEM((1, rows), jnp.int32),
            pltpu.VMEM((1, rows), jnp.int32),
            pltpu.VMEM((fdev + 2, hdev + 2, width, chans), jnp.bfloat16),
            pltpu.VMEM((3, 3, chans, 3 * chans), jnp.bfloat16),
            pltpu.VMEM((2, 3, chans, 3 * chans), jnp.bfloat16),
            pltpu.VMEM((held * pitch, chans), jnp.float32),
            pltpu.VMEM((chans // l2 * chans, chans), jnp.bfloat16),
            pltpu.VMEM((n_tm * slots_per, held), jnp.bfloat16),
            pltpu.VMEM((2, 8, chans), jnp.float32),
            pltpu.VMEM((n, 8, chans), jnp.float32),
            pltpu.VMEM((1, chans), jnp.float32),
            pltpu.VMEM((n_tm, cap, lat), jnp.bfloat16),
            pltpu.VMEM((n_tm, capb, lat), jnp.bfloat16),
            pltpu.VMEM((n_tm, capb, lat), jnp.bfloat16),
            pltpu.SemaphoreType.DMA((10,)),
            pltpu.SemaphoreType.DMA((15,)),
            pltpu.SemaphoreType.DMA((15,)),
            pltpu.SemaphoreType.DMA((n,)),
            pltpu.SemaphoreType.DMA((n,)),
            *[pltpu.SemaphoreType.DMA((chunks, n_tm))] * 4,
            pltpu.SemaphoreType.REGULAR((2,)),
        ],
        compiler_params=pltpu.CompilerParams(
            collective_id=0, has_side_effects=True, vmem_limit_bytes=VMEM - kept_bytes
        ),
    )(
        frame_counts.reshape(1, 1),
        video[0],
        conv_weight,
        norm_gain.reshape(1, chans),
        norm_shift.reshape(1, chans),
        quant_weight.T,
        quant_bias.reshape(1, l2),
        row_dest.reshape(1, rows),
    )
    return out.reshape(1, 1, 1, n_tm, cap, lat)


def solution(mesh):
    return jax.shard_map(
        functools.partial(body, mesh.shape["tm"], mesh.shape["space"]),
        mesh=mesh,
        in_specs=(
            P("clip", "tm", "space", None, None),
            P("clip"),
            P(),
            P(),
            P(),
            P(),
            P(),
            P("clip", "tm", "space", None, None),
        ),
        out_specs=P("clip", "tm", "space", None, None, None),
        check_vma=False,
    )
```

```python
import functools

import jax
import jax.numpy as jnp
from jax import lax
from jax.experimental import pallas as pl
from jax.experimental.pallas import tpu as pltpu
from jax.sharding import PartitionSpec as P

GROUPS = 32
MESH = pl.DeviceIdType.MESH
TILES = 8
VMEM = 64 * 1024 * 1024


def kernel(
    n_tm,
    n_space,
    cap,
    capb,
    own_slots,
    slots_per,
    pitch,
    count_hbm,
    video,
    weight,
    gain_hbm,
    shift_hbm,
    qw_hbm,
    qb_hbm,
    dest_hbm,
    out,
    count_ref,
    gain_ref,
    shift_ref,
    qw_ref,
    qb_ref,
    dest_ref,
    next_ref,
    xs,
    wb,
    folded_taps,
    act,
    wq,
    place,
    stats,
    gathered,
    bias_ref,
    outgoing,
    extra,
    extra_in,
    local_sem,
    halo_send,
    halo_recv,
    stat_send,
    stat_recv,
    row_send,
    row_recv,
    extra_send,
    extra_recv,
    token_sem,
):
    fdev, hdev, width, chans = video.shape
    l2 = qw_ref.shape[0]
    rows = fdev * hdev
    held = place.shape[1]
    folded = chans // l2
    lat = width * l2
    n = n_tm * n_space
    tm, space = lax.axis_index("tm"), lax.axis_index("space")
    me = tm * n_space + space
    first_tm, last_tm = tm == 0, tm == n_tm - 1

    def at(peer):
        return {"tm": peer // n_space, "space": lax.rem(peer, n_space)}

    barrier = pltpu.get_barrier_semaphore()

    near = n_tm == 2
    later = {"tm": lax.rem(tm + 1, n_tm)}
    earlier = {"tm": lax.rem(tm + n_tm - 1, n_tm)}
    above = {"space": lax.rem(space + n_space - 1, n_space)}
    below = {"space": lax.rem(space + 1, n_space)}

    def tell(sem, device):
        pl.semaphore_signal(sem, inc=1, device_id=device, device_id_type=MESH)

    if near:
        tell(barrier, later)

        @pl.when(space > 0)
        def _():
            tell(barrier, above)

        @pl.when(space < n_space - 1)
        def _():
            tell(barrier, below)

    else:

        @pl.loop(1, n)
        def _(step):
            tell(barrier, at(lax.rem(me + step, n)))

    taps = [
        pltpu.make_async_copy(
            weight.at[:, :, dw],
            wb.at[:, :, :, pl.ds(dw * chans, chans)],
            local_sem.at[1 + dw],
        )
        for dw in range(3)
    ]
    for tap in taps:
        tap.start()
    own = pltpu.make_async_copy(
        video, xs.at[pl.ds(1, fdev), pl.ds(1, hdev)], local_sem.at[0]
    )
    own.start()

    smalls = [
        pltpu.make_async_copy(src, dst, local_sem.at[4 + i])
        for i, (src, dst) in enumerate(
            [
                (qw_hbm, qw_ref),
                (qb_hbm, qb_ref),
                (dest_hbm, dest_ref),
                (gain_hbm, gain_ref),
                (shift_hbm, shift_ref),
                (count_hbm, count_ref),
            ]
        )
    ]
    for small in smalls:
        small.start()

    def prepare():
        zero_row = jnp.zeros((fdev + 2, width, chans), jnp.bfloat16)

        @pl.when(space == 0)
        def _():
            xs[:, 0] = zero_row

        @pl.when(space == n_space - 1)
        def _():
            xs[:, hdev + 1] = zero_row

        zero_frame = jnp.zeros((hdev * pitch, chans), jnp.float32)

        @pl.when(tm > 0)
        def _():
            act[pl.ds(0, hdev * pitch), :] = zero_frame

        @pl.when(tm == n_tm - 1)
        def _():
            act[pl.ds(rows * pitch, hdev * pitch), :] = zero_frame

        spare = held - rows - hdev
        act[pl.ds((rows + hdev) * pitch, spare * pitch), :] = jnp.zeros(
            (spare * pitch, chans), jnp.float32
        )

        for small in smalls:
            small.wait()
        lane = lax.broadcasted_iota(jnp.int32, (l2, chans), 1)
        sub = lax.broadcasted_iota(jnp.int32, (l2, chans), 0)
        spread = jnp.zeros((l2, chans), jnp.float32)
        for i in range(folded):
            pick = jnp.where(lane == sub + i * l2, 1.0, 0.0)
            spread = spread + pick
            wq[pl.ds(i * chans, chans), :] = lax.dot_general(
                qw_ref[...],
                pick.astype(jnp.bfloat16),
                (((0,), (0,)), ((), ())),
                preferred_element_type=jnp.float32,
            ).astype(jnp.bfloat16)
        bias_ref[...] = jnp.dot(
            qb_ref[...],
            spread,
            precision=lax.Precision.HIGHEST,
            preferred_element_type=jnp.float32,
        )
        stats[...] = jnp.zeros_like(stats)

    @pl.when(tm == 0)
    def _():
        prepare()

    if near:
        outer = (space == 0) | (space == n_space - 1)

        @pl.when(outer)
        def _():
            pl.semaphore_wait(barrier, min(n_space, 2))

        @pl.when(~outer)
        def _():
            pl.semaphore_wait(barrier, 3)

    else:
        pl.semaphore_wait(barrier, n - 1)

    def token(hop):
        if not near:
            return

        @pl.when(space == hop)
        def _():
            if hop > 0:
                pl.semaphore_wait(token_sem.at[0], 1)
            if hop < n_space - 1:
                tell(token_sem.at[0], below)

        @pl.when(space == n_space - 1 - hop)
        def _():
            if hop > 0:
                pl.semaphore_wait(token_sem.at[1], 1)
            if hop < n_space - 1:
                tell(token_sem.at[1], above)

    def remote(src, dst, index, device):
        return pltpu.make_async_remote_copy(
            src_ref=src,
            dst_ref=dst,
            send_sem=halo_send.at[index],
            recv_sem=halo_recv.at[index],
            device_id=device,
            device_id_type=MESH,
        )

    after = fdev + 1

    def frame_copies(source, target, index, device):
        return [
            remote(video.at[source, 0], xs.at[target, 1], index, device),
            remote(video.at[source, hdev - 1], xs.at[target, hdev], index + 1, device),
            remote(
                video.at[source, pl.ds(1, hdev - 2)],
                xs.at[target, pl.ds(2, hdev - 2)],
                index + 2,
                device,
            ),
        ]

    def corner_copies(target, index):
        return [
            remote(xs.at[target, 1], xs.at[target, hdev + 1], index, above),
            remote(xs.at[target, hdev], xs.at[target, 0], index + 1, below),
        ]

    forward = frame_copies(fdev - 1, 0, 0, later)
    back = frame_copies(0, after, 3, earlier)
    forward_corners = corner_copies(0, 6)
    back_corners = corner_copies(after, 8)
    half = fdev // 2

    def row_halo(start, count, index):
        source, target = pl.ds(start, count), pl.ds(start + 1, count)
        return [
            remote(video.at[source, 0], xs.at[target, hdev + 1], index, above),
            remote(video.at[source, hdev - 1], xs.at[target, 0], index + 1, below),
        ]

    early_rows, late_rows = row_halo(0, half, 10), row_halo(half, fdev - half, 13)
    dest_copy = remote(dest_hbm, next_ref, 12, earlier)

    second = lax.rem(lax.axis_index("clip"), 2) == 1

    def send_frames():
        @pl.when(tm > 0)
        def _():
            for copy in back:
                copy.start()

        @pl.when(tm < n_tm - 1)
        def _():
            for copy in forward:
                copy.start()

    def send_rows():
        @pl.when(space > 0)
        def _():
            early_rows[0].start()
            late_rows[0].start()

        @pl.when(space < n_space - 1)
        def _():
            early_rows[1].start()
            late_rows[1].start()

    @pl.when(~second)
    def _():
        send_rows()
        send_frames()

    @pl.when(second)
    def _():
        send_frames()
        send_rows()

    @pl.when(tm > 0)
    def _():
        dest_copy.start()

    token(0)

    @pl.when(tm > 0)
    def _():
        prepare()

    count = count_ref[...]

    def valid(frame):
        ids = jnp.full((1, chans), 0, jnp.int32) + (tm * fdev + frame)
        return jnp.where(ids < count, 1.0, 0.0)

    cell = lax.broadcasted_iota(jnp.int32, (width, chans), 0)

    def accumulate(fs, taps_of, fresh, final, hs):
        items = [(f, h) for f in fs for h in hs]
        m = len(items) * width

        def index(f, dt):
            p = f - 1 + dt
            return 1 if p == 0 and len(taps_of) == 3 else p

        if fs == [0]:
            frames_of = [[1], [1]]
            kernel_part = folded_taps[...].reshape(-1, 3 * chans)
        else:
            frames_of = [[index(f, dt) for f in fs] for dt in taps_of]
            kernel_part = wb[pl.ds(taps_of[0], len(taps_of))].reshape(-1, 3 * chans)
        pieces = [
            jnp.concatenate([xs[p, h + dh] for p in ps for h in hs], axis=0)
            for ps in frames_of
            for dh in range(3)
        ]
        y = jnp.dot(
            jnp.concatenate(pieces, axis=1), kernel_part, preferred_element_type=jnp.float32
        )
        for i, (f, h) in enumerate(items):
            part = y[i * width : (i + 1) * width]
            before = pltpu.roll(part[:, :chans], 1, 0)
            after_ = pltpu.roll(part[:, 2 * chans :], width - 1, 0)
            total = (
                part[:, chans : 2 * chans]
                + jnp.where(cell == 0, 0.0, before)
                + jnp.where(cell == width - 1, 0.0, after_)
            )
            spot = pl.ds((f * hdev + h) * pitch, width)
            if not fresh:
                total = total + act[spot, :]
            if final:
                total = total * valid(f)
                stats[0] += jnp.sum(total.reshape(width // 8, 8, chans), axis=0)
                stats[1] += jnp.sum((total * total).reshape(width // 8, 8, chans), axis=0)
            act[spot, :] = total

    inner, edge = list(range(1, hdev - 1)), [0, hdev - 1]

    @pl.when(tm == 0)
    def _():
        for tap in taps:
            tap.wait()

        @pl.loop(0, 3)
        def _(dh):
            total = sum(wb[dt, dh].astype(jnp.float32) for dt in range(3))
            high = total.astype(jnp.bfloat16)
            folded_taps[0, dh] = high
            folded_taps[1, dh] = (total - high.astype(jnp.float32)).astype(jnp.bfloat16)

    own.wait()

    @pl.when(tm > 0)
    def _():
        for tap in taps:
            tap.wait()

    def pass_corners(arrived, corners):
        arrived[0].wait_recv()
        arrived[1].wait_recv()

        @pl.when(space > 0)
        def _():
            corners[0].start()

        @pl.when(space < n_space - 1)
        def _():
            corners[1].start()

    @pl.when(tm == 0)
    def _():
        accumulate(range(1, fdev), (0, 1, 2), True, True, inner)
        accumulate([0], (0, 1, 2), True, True, inner)

    @pl.when(tm > 0)
    def _():
        accumulate(range(2, fdev), (0, 1, 2), True, True, inner)
        pass_corners(forward, forward_corners)
        accumulate([1], (1, 2), True, False, inner)

    @pl.when(tm < n_tm - 1)
    def _():
        pass_corners(back, back_corners)
        accumulate([fdev], (0, 1), True, False, inner)

    if n_space > 2:
        token(1)

    def rows_in(copies):
        @pl.when(space < n_space - 1)
        def _():
            copies[0].wait_recv()

        @pl.when(space > 0)
        def _():
            copies[1].wait_recv()

    rows_in(early_rows)

    @pl.when(tm == 0)
    def _():
        accumulate(range(1, half), (0, 1, 2), True, True, edge)
        accumulate([0], (0, 1, 2), True, True, edge)

    rows_in(late_rows)

    @pl.when(tm == 0)
    def _():
        accumulate(range(half, fdev), (0, 1, 2), True, True, edge)

    @pl.when(tm > 0)
    def _():
        accumulate(range(2, fdev), (0, 1, 2), True, True, edge)
        accumulate([1], (1, 2), True, False, edge)

    @pl.when(tm < n_tm - 1)
    def _():
        accumulate([fdev], (0, 1), True, False, edge)

    for hop in range(2, n_space - 1):
        token(hop)

    def corners_in(corners):
        @pl.when(space < n_space - 1)
        def _():
            corners[0].wait_recv()

        @pl.when(space > 0)
        def _():
            corners[1].wait_recv()

    @pl.when(tm > 0)
    def _():
        corners_in(forward_corners)
        forward[2].wait_recv()
        accumulate([1], (0,), False, True, range(hdev))

    @pl.when(tm < n_tm - 1)
    def _():
        back[2].wait_recv()
        accumulate([fdev], (2,), False, True, inner)
        corners_in(back_corners)
        accumulate([fdev], (2,), False, True, edge)

    halves = [jnp.sum(stats[i], axis=0, keepdims=True) for i in range(2)]
    line = lax.broadcasted_iota(jnp.int32, (8, chans), 0)
    gathered[me] = jnp.where(line == 0, halves[0], jnp.where(line == 1, halves[1], 0.0))

    def stat_copy(step):
        return pltpu.make_async_remote_copy(
            src_ref=gathered.at[me],
            dst_ref=gathered.at[me],
            send_sem=stat_send.at[step],
            recv_sem=stat_recv.at[me],
            device_id=at(lax.rem(me + step, n)),
            device_id_type=MESH,
        )

    def stat_arrival(step):
        sender = lax.rem(me + step, n)
        return pltpu.make_async_remote_copy(
            src_ref=gathered.at[sender],
            dst_ref=gathered.at[sender],
            send_sem=stat_send.at[step],
            recv_sem=stat_recv.at[sender],
            device_id=at(sender),
            device_id_type=MESH,
        )

    if n_space > 1:
        token(n_space - 1)

    @pl.loop(1, n)
    def _(step):
        stat_copy(step).start()

    @pl.when(tm < n_tm - 1)
    def _():
        dest_copy.wait_recv()

    @pl.when(tm == n_tm - 1)
    def _():
        next_ref[...] = jnp.zeros_like(next_ref)

    def numbers(shape, axis):
        return lax.broadcasted_iota(jnp.int32, shape, axis)

    along, across = numbers((held, held), 0), numbers((held, held), 1)
    source, column = numbers((rows, held), 0), numbers((rows, held), 1)
    named = jnp.dot(
        dest_ref[...].astype(jnp.float32),
        jnp.where(source == column, 1.0, 0.0),
        precision=lax.Precision.HIGHEST,
        preferred_element_type=jnp.float32,
    ) + jnp.dot(
        next_ref[...].astype(jnp.float32),
        jnp.where((source + rows == column) & (source < hdev), 1.0, 0.0),
        precision=lax.Precision.HIGHEST,
        preferred_element_type=jnp.float32,
    )
    wide_named = jnp.broadcast_to(named, (held, held))
    tall_named = jnp.sum(jnp.where(across == along, wide_named, 0.0), axis=1, keepdims=True)
    alike = (tall_named == wide_named) & (along < across) & ((along < rows) == (across < rows))
    rank = jnp.sum(jnp.where(alike, 1.0, 0.0), axis=0, keepdims=True)
    position = numbers((1, held), 1)
    here = (
        ((position < hdev) & first_tm)
        | ((position >= hdev) & (position < rows))
        | ((position >= rows) & (position < rows + hdev) & (~last_tm))
    )
    slot = named * slots_per + rank + jnp.where(position >= rows, 1.0 * own_slots, 0.0)
    slot = jnp.where(here, slot, -1.0)
    slots = numbers((place.shape[0], held), 0).astype(jnp.float32)
    place[...] = jnp.where(slots == slot, 1.0, 0.0).astype(jnp.bfloat16)

    @pl.loop(1, n)
    def _(step):
        stat_arrival(step).wait_recv()

    sums = jnp.sum(gathered[...], axis=0)
    position = lax.broadcasted_iota(jnp.int32, (8, chans), 1)
    per = chans // GROUPS
    reach = 1
    while reach < per:
        low = lax.rem(position // reach, 2) == 0
        sums = sums + jnp.where(
            low, pltpu.roll(sums, chans - reach, 1), pltpu.roll(sums, reach, 1)
        )
        reach *= 2
    amount = jnp.full((1, chans), 1, jnp.int32) * count
    total_count = amount.astype(jnp.float32) * (n_space * hdev * width * per)
    mean = sums[0:1] / total_count
    var = jnp.maximum(sums[1:2] / total_count - mean * mean, 0.0)
    scale = lax.rsqrt(var + 1e-06) * gain_ref[...]
    offset = shift_ref[...] - mean * scale
    scale, offset = 0.5 * scale, 0.5 * offset
    row = numbers((held, chans), 0)
    frame = jnp.zeros((held, chans), jnp.int32) + tm * fdev
    for f in range(1, fdev + 1):
        frame = frame + jnp.where(row >= f * hdev, 1, 0)
    frame_masks = jnp.where(frame < count, 1.0, 0.0)
    chunks = lat // (TILES * chans)

    wide_cells = TILES * chans

    def columns(chunk):
        return pl.ds(pl.multiple_of(chunk * wide_cells, wide_cells), wide_cells)

    def row_copies(chunk, step, sender):
        peer = lax.rem(tm + step, n_tm)
        place_of = peer if sender else tm
        return [
            pltpu.make_async_remote_copy(
                src_ref=source.at[peer, :, columns(chunk)],
                dst_ref=target.at[place_of, :, columns(chunk)],
                send_sem=send.at[chunk, step],
                recv_sem=recv.at[chunk, place_of],
                device_id={"tm": peer},
                device_id_type=MESH,
            )
            for source, target, send, recv in [
                (outgoing, out, row_send, row_recv),
                (extra, extra_in, extra_send, extra_recv),
            ]
        ]

    @functools.partial(lax.fori_loop, 0, chunks, init_val=None, unroll=True)
    def _(chunk, _carry):
        hidden = []
        for j in range(TILES):
            cells = []
            for i in range(folded):
                w = (chunk * TILES + j) * folded + i
                half = act[pl.ds(w, held, stride=pitch), :] * scale + offset
                cells.append((half + half * jnp.tanh(half)) * frame_masks)
            hidden.append(jnp.concatenate(cells, axis=1))
        hidden = jnp.concatenate(hidden, axis=0).astype(jnp.bfloat16)
        moments = (
            jnp.dot(hidden, wq[...], preferred_element_type=jnp.float32) + bias_ref[...]
        )
        wide = jnp.concatenate(
            [moments[j * held : (j + 1) * held] for j in range(TILES)], axis=1
        ).astype(jnp.bfloat16)
        routed = jnp.dot(place[...], wide, preferred_element_type=jnp.float32)
        for d in range(n_tm):
            start = d * slots_per
            outgoing[d, :, columns(chunk)] = routed[start : start + cap].astype(jnp.bfloat16)
            start = start + own_slots
            extra[d, :, columns(chunk)] = routed[start : start + capb].astype(jnp.bfloat16)

        @pl.loop(1, n_tm)
        def _(step):
            own, more = row_copies(chunk, step, False)
            own.start()

            @pl.when(tm < n_tm - 1)
            def _():
                more.start()

        mine = jnp.dot(
            place[pl.ds(pl.multiple_of(tm * slots_per, slots_per), slots_per), :],
            wide,
            preferred_element_type=jnp.float32,
        )
        out[tm, :, columns(chunk)] = mine[:cap].astype(jnp.bfloat16)
        extra_in[tm, :, columns(chunk)] = mine[own_slots : own_slots + capb].astype(
            jnp.bfloat16
        )

    @pl.loop(1, n)
    def _(step):
        stat_copy(step).wait_send()

    def sent(corners):
        @pl.when(space > 0)
        def _():
            corners[0].wait_send()

        @pl.when(space < n_space - 1)
        def _():
            corners[1].wait_send()

    @pl.when(tm < n_tm - 1)
    def _():
        for copy in forward:
            copy.wait_send()
        sent(back_corners)

    @pl.when(tm > 0)
    def _():
        for copy in back:
            copy.wait_send()
        dest_copy.wait_send()
        sent(forward_corners)

    @pl.when(space > 0)
    def _():
        early_rows[0].wait_send()
        late_rows[0].wait_send()

    @pl.when(space < n_space - 1)
    def _():
        early_rows[1].wait_send()
        late_rows[1].wait_send()

    @pl.loop(0, chunks)
    def _(chunk):
        @pl.loop(1, n_tm)
        def _(step):
            own, more = row_copies(chunk, step, False)
            own.wait_send()

            @pl.when(tm < n_tm - 1)
            def _():
                more.wait_send()

            own, more = row_copies(chunk, step, True)
            own.wait_recv()

            @pl.when(lax.rem(tm + step, n_tm) < n_tm - 1)
            def _():
                more.wait_recv()

        @pl.loop(1, n_tm)
        def _(t):
            out[t, :capb, columns(chunk)] = (
                out[t, :capb, columns(chunk)].astype(jnp.float32)
                + extra_in[t - 1, :, columns(chunk)].astype(jnp.float32)
            ).astype(jnp.bfloat16)


def hand_over(source, target, sem):
    copy = pltpu.make_async_copy(source, target, sem)
    copy.start()
    copy.wait()


def body(
    n_tm,
    n_space,
    video,
    frame_counts,
    conv_weight,
    norm_gain,
    norm_shift,
    quant_weight,
    quant_bias,
    row_dest,
):
    clips, fdev, hdev, width, chans = video.shape
    l2 = quant_weight.shape[1]
    rows = fdev * hdev
    lat = width * l2
    cap = min(max(2, 2 * rows // n_tm), rows)
    capb = min(cap, hdev)
    own_slots = -(-cap // 8) * 8
    slots_per = own_slots + -(-capb // 8) * 8
    held = -(-(rows + hdev) // 16) * 16
    pitch = width + 8
    n = n_tm * n_space
    chunks = lat // (TILES * chans)
    kept_bytes = n_tm * own_slots * lat * 2 + 128 * 1024
    hbm = pl.BlockSpec(memory_space=pltpu.HBM)
    out = pl.pallas_call(
        functools.partial(kernel, n_tm, n_space, cap, capb, own_slots, slots_per, pitch),
        out_shape=pltpu.VMEM((n_tm, cap, lat), jnp.bfloat16),
        in_specs=[hbm] * 8,
        out_specs=pl.BlockSpec(memory_space=pltpu.VMEM),
        scratch_shapes=[
            pltpu.VMEM((1, 1), jnp.int32),
            pltpu.VMEM((1, chans), jnp.float32),
            pltpu.VMEM((1, chans), jnp.float32),
            pltpu.VMEM((l2, chans), jnp.bfloat16),
            pltpu.VMEM((1, l2), jnp.float32),
            pltpu.VMEM((1, rows), jnp.int32),
            pltpu.VMEM((1, rows), jnp.int32),
            pltpu.VMEM((fdev + 2, hdev + 2, width, chans), jnp.bfloat16),
            pltpu.VMEM((3, 3, chans, 3 * chans), jnp.bfloat16),
            pltpu.VMEM((2, 3, chans, 3 * chans), jnp.bfloat16),
            pltpu.VMEM((held * pitch, chans), jnp.float32),
            pltpu.VMEM((chans // l2 * chans, chans), jnp.bfloat16),
            pltpu.VMEM((n_tm * slots_per, held), jnp.bfloat16),
            pltpu.VMEM((2, 8, chans), jnp.float32),
            pltpu.VMEM((n, 8, chans), jnp.float32),
            pltpu.VMEM((1, chans), jnp.float32),
            pltpu.VMEM((n_tm, cap, lat), jnp.bfloat16),
            pltpu.VMEM((n_tm, capb, lat), jnp.bfloat16),
            pltpu.VMEM((n_tm, capb, lat), jnp.bfloat16),
            pltpu.SemaphoreType.DMA((10,)),
            pltpu.SemaphoreType.DMA((15,)),
            pltpu.SemaphoreType.DMA((15,)),
            pltpu.SemaphoreType.DMA((n,)),
            pltpu.SemaphoreType.DMA((n,)),
            *[pltpu.SemaphoreType.DMA((chunks, n_tm))] * 4,
            pltpu.SemaphoreType.REGULAR((2,)),
        ],
        compiler_params=pltpu.CompilerParams(
            collective_id=0, has_side_effects=True, vmem_limit_bytes=VMEM - kept_bytes
        ),
    )(
        frame_counts.reshape(1, 1),
        video[0],
        conv_weight,
        norm_gain.reshape(1, chans),
        norm_shift.reshape(1, chans),
        quant_weight.T,
        quant_bias.reshape(1, l2),
        row_dest.reshape(1, rows),
    )
    return out.reshape(1, 1, 1, n_tm, cap, lat)


def solution(mesh):
    return jax.shard_map(
        functools.partial(body, mesh.shape["tm"], mesh.shape["space"]),
        mesh=mesh,
        in_specs=(
            P("clip", "tm", "space", None, None),
            P("clip"),
            P(),
            P(),
            P(),
            P(),
            P(),
            P("clip", "tm", "space", None, None),
        ),
        out_specs=P("clip", "tm", "space", None, None, None),
        check_vma=False,
    )
```

```python
import functools

import jax
import jax.numpy as jnp
from jax import lax
from jax.experimental import pallas as pl
from jax.experimental.pallas import tpu as pltpu
from jax.sharding import PartitionSpec as P

GROUPS = 32
MESH = pl.DeviceIdType.MESH
TILES = 8
VMEM = 64 * 1024 * 1024


def kernel(
    n_tm,
    n_space,
    cap,
    capb,
    own_slots,
    slots_per,
    pitch,
    count_hbm,
    video,
    weight,
    gain_hbm,
    shift_hbm,
    qw_hbm,
    qb_hbm,
    dest_hbm,
    out,
    count_ref,
    gain_ref,
    shift_ref,
    qw_ref,
    qb_ref,
    dest_ref,
    next_ref,
    xs,
    wb,
    folded_taps,
    act,
    wq,
    place,
    stats,
    gathered,
    bias_ref,
    outgoing,
    extra,
    extra_in,
    local_sem,
    halo_send,
    halo_recv,
    stat_send,
    stat_recv,
    row_send,
    row_recv,
    extra_send,
    extra_recv,
    token_sem,
):
    fdev, hdev, width, chans = video.shape
    l2 = qw_ref.shape[0]
    rows = fdev * hdev
    held = place.shape[1]
    folded = chans // l2
    lat = width * l2
    n = n_tm * n_space
    tm, space = lax.axis_index("tm"), lax.axis_index("space")
    me = tm * n_space + space
    first_tm, last_tm = tm == 0, tm == n_tm - 1

    def at(peer):
        return {"tm": peer // n_space, "space": lax.rem(peer, n_space)}

    barrier = pltpu.get_barrier_semaphore()

    near = n_tm == 2
    later = {"tm": lax.rem(tm + 1, n_tm)}
    earlier = {"tm": lax.rem(tm + n_tm - 1, n_tm)}
    above = {"space": lax.rem(space + n_space - 1, n_space)}
    below = {"space": lax.rem(space + 1, n_space)}

    def tell(sem, device):
        pl.semaphore_signal(sem, inc=1, device_id=device, device_id_type=MESH)

    if near:
        tell(barrier, later)

        @pl.when(space > 0)
        def _():
            tell(barrier, above)

        @pl.when(space < n_space - 1)
        def _():
            tell(barrier, below)

    else:

        @pl.loop(1, n)
        def _(step):
            tell(barrier, at(lax.rem(me + step, n)))

    taps = [
        pltpu.make_async_copy(
            weight.at[:, :, dw],
            wb.at[:, :, :, pl.ds(dw * chans, chans)],
            local_sem.at[1 + dw],
        )
        for dw in range(3)
    ]
    for tap in taps:
        tap.start()
    own = pltpu.make_async_copy(
        video, xs.at[pl.ds(1, fdev), pl.ds(1, hdev)], local_sem.at[0]
    )
    own.start()

    smalls = [
        pltpu.make_async_copy(src, dst, local_sem.at[4 + i])
        for i, (src, dst) in enumerate(
            [
                (qw_hbm, qw_ref),
                (qb_hbm, qb_ref),
                (dest_hbm, dest_ref),
                (gain_hbm, gain_ref),
                (shift_hbm, shift_ref),
                (count_hbm, count_ref),
            ]
        )
    ]
    for small in smalls:
        small.start()

    def prepare():
        zero_row = jnp.zeros((fdev + 2, width, chans), jnp.bfloat16)

        @pl.when(space == 0)
        def _():
            xs[:, 0] = zero_row

        @pl.when(space == n_space - 1)
        def _():
            xs[:, hdev + 1] = zero_row

        zero_frame = jnp.zeros((hdev * pitch, chans), jnp.float32)

        @pl.when(tm > 0)
        def _():
            act[pl.ds(0, hdev * pitch), :] = zero_frame

        @pl.when(tm == n_tm - 1)
        def _():
            act[pl.ds(rows * pitch, hdev * pitch), :] = zero_frame

        spare = held - rows - hdev
        act[pl.ds((rows + hdev) * pitch, spare * pitch), :] = jnp.zeros(
            (spare * pitch, chans), jnp.float32
        )

        for small in smalls:
            small.wait()
        lane = lax.broadcasted_iota(jnp.int32, (l2, chans), 1)
        sub = lax.broadcasted_iota(jnp.int32, (l2, chans), 0)
        spread = jnp.zeros((l2, chans), jnp.float32)
        for i in range(folded):
            pick = jnp.where(lane == sub + i * l2, 1.0, 0.0)
            spread = spread + pick
            wq[pl.ds(i * chans, chans), :] = lax.dot_general(
                qw_ref[...],
                pick.astype(jnp.bfloat16),
                (((0,), (0,)), ((), ())),
                preferred_element_type=jnp.float32,
            ).astype(jnp.bfloat16)
        bias_ref[...] = jnp.dot(
            qb_ref[...],
            spread,
            precision=lax.Precision.HIGHEST,
            preferred_element_type=jnp.float32,
        )
        stats[...] = jnp.zeros_like(stats)

    @pl.when(tm == 0)
    def _():
        prepare()

    if near:
        outer = (space == 0) | (space == n_space - 1)

        @pl.when(outer)
        def _():
            pl.semaphore_wait(barrier, min(n_space, 2))

        @pl.when(~outer)
        def _():
            pl.semaphore_wait(barrier, 3)

    else:
        pl.semaphore_wait(barrier, n - 1)

    def token(hop):
        if not near:
            return

        @pl.when(space == hop)
        def _():
            if hop > 0:
                pl.semaphore_wait(token_sem.at[0], 1)
            if hop < n_space - 1:
                tell(token_sem.at[0], below)

        @pl.when(space == n_space - 1 - hop)
        def _():
            if hop > 0:
                pl.semaphore_wait(token_sem.at[1], 1)
            if hop < n_space - 1:
                tell(token_sem.at[1], above)

    def remote(src, dst, index, device):
        return pltpu.make_async_remote_copy(
            src_ref=src,
            dst_ref=dst,
            send_sem=halo_send.at[index],
            recv_sem=halo_recv.at[index],
            device_id=device,
            device_id_type=MESH,
        )

    after = fdev + 1

    def frame_copies(source, target, index, device):
        return [
            remote(video.at[source, 0], xs.at[target, 1], index, device),
            remote(video.at[source, hdev - 1], xs.at[target, hdev], index + 1, device),
            remote(
                video.at[source, pl.ds(1, hdev - 2)],
                xs.at[target, pl.ds(2, hdev - 2)],
                index + 2,
                device,
            ),
        ]

    def corner_copies(target, index):
        return [
            remote(xs.at[target, 1], xs.at[target, hdev + 1], index, above),
            remote(xs.at[target, hdev], xs.at[target, 0], index + 1, below),
        ]

    forward = frame_copies(fdev - 1, 0, 0, later)
    back = frame_copies(0, after, 3, earlier)
    forward_corners = corner_copies(0, 6)
    back_corners = corner_copies(after, 8)
    half = fdev // 2

    def row_halo(start, count, index):
        source, target = pl.ds(start, count), pl.ds(start + 1, count)
        return [
            remote(video.at[source, 0], xs.at[target, hdev + 1], index, above),
            remote(video.at[source, hdev - 1], xs.at[target, 0], index + 1, below),
        ]

    early_rows, late_rows = row_halo(0, half, 10), row_halo(half, fdev - half, 13)
    dest_copy = remote(dest_hbm, next_ref, 12, earlier)

    second = lax.rem(lax.axis_index("clip"), 2) == 1

    def send_frames():
        @pl.when(tm > 0)
        def _():
            for copy in back:
                copy.start()

        @pl.when(tm < n_tm - 1)
        def _():
            for copy in forward:
                copy.start()

    def send_rows():
        @pl.when(space > 0)
        def _():
            early_rows[0].start()
            late_rows[0].start()

        @pl.when(space < n_space - 1)
        def _():
            early_rows[1].start()
            late_rows[1].start()

    @pl.when(~second)
    def _():
        send_rows()
        send_frames()

    @pl.when(second)
    def _():
        send_frames()
        send_rows()

    @pl.when(tm > 0)
    def _():
        dest_copy.start()

    token(0)

    @pl.when(tm > 0)
    def _():
        prepare()

    count = count_ref[...]

    def valid(frame):
        ids = jnp.full((1, chans), 0, jnp.int32) + (tm * fdev + frame)
        return jnp.where(ids < count, 1.0, 0.0)

    cell = lax.broadcasted_iota(jnp.int32, (width, chans), 0)

    def accumulate(fs, taps_of, fresh, final, hs):
        items = [(f, h) for f in fs for h in hs]
        m = len(items) * width

        def index(f, dt):
            p = f - 1 + dt
            return 1 if p == 0 and len(taps_of) == 3 else p

        if fs == [0]:
            frames_of = [[1], [1]]
            kernel_part = folded_taps[...].reshape(-1, 3 * chans)
        else:
            frames_of = [[index(f, dt) for f in fs] for dt in taps_of]
            kernel_part = wb[pl.ds(taps_of[0], len(taps_of))].reshape(-1, 3 * chans)
        pieces = [
            jnp.concatenate([xs[p, h + dh] for p in ps for h in hs], axis=0)
            for ps in frames_of
            for dh in range(3)
        ]
        y = jnp.dot(
            jnp.concatenate(pieces, axis=1), kernel_part, preferred_element_type=jnp.float32
        )
        for i, (f, h) in enumerate(items):
            part = y[i * width : (i + 1) * width]
            before = pltpu.roll(part[:, :chans], 1, 0)
            after_ = pltpu.roll(part[:, 2 * chans :], width - 1, 0)
            total = (
                part[:, chans : 2 * chans]
                + jnp.where(cell == 0, 0.0, before)
                + jnp.where(cell == width - 1, 0.0, after_)
            )
            spot = pl.ds((f * hdev + h) * pitch, width)
            if not fresh:
                total = total + act[spot, :]
            if final:
                total = total * valid(f)
                stats[0] += jnp.sum(total.reshape(width // 8, 8, chans), axis=0)
                stats[1] += jnp.sum((total * total).reshape(width // 8, 8, chans), axis=0)
            act[spot, :] = total

    inner, edge = list(range(1, hdev - 1)), [0, hdev - 1]

    @pl.when(tm == 0)
    def _():
        for tap in taps:
            tap.wait()

        @pl.loop(0, 3)
        def _(dh):
            total = sum(wb[dt, dh].astype(jnp.float32) for dt in range(3))
            high = total.astype(jnp.bfloat16)
            folded_taps[0, dh] = high
            folded_taps[1, dh] = (total - high.astype(jnp.float32)).astype(jnp.bfloat16)

    own.wait()

    @pl.when(tm > 0)
    def _():
        for tap in taps:
            tap.wait()

    def pass_corners(arrived, corners):
        arrived[0].wait_recv()
        arrived[1].wait_recv()

        @pl.when(space > 0)
        def _():
            corners[0].start()

        @pl.when(space < n_space - 1)
        def _():
            corners[1].start()

    @pl.when(tm == 0)
    def _():
        accumulate(range(1, fdev), (0, 1, 2), True, True, inner)
        accumulate([0], (0, 1, 2), True, True, inner)

    @pl.when(tm > 0)
    def _():
        accumulate(range(2, fdev), (0, 1, 2), True, True, inner)
        pass_corners(forward, forward_corners)
        accumulate([1], (1, 2), True, False, inner)

    @pl.when(tm < n_tm - 1)
    def _():
        pass_corners(back, back_corners)
        accumulate([fdev], (0, 1), True, False, inner)

    if n_space > 2:
        token(1)

    def rows_in(copies):
        @pl.when(space < n_space - 1)
        def _():
            copies[0].wait_recv()

        @pl.when(space > 0)
        def _():
            copies[1].wait_recv()

    rows_in(early_rows)

    @pl.when(tm == 0)
    def _():
        accumulate(range(1, half), (0, 1, 2), True, True, edge)
        accumulate([0], (0, 1, 2), True, True, edge)

    rows_in(late_rows)

    @pl.when(tm == 0)
    def _():
        accumulate(range(half, fdev), (0, 1, 2), True, True, edge)

    @pl.when(tm > 0)
    def _():
        accumulate(range(2, fdev), (0, 1, 2), True, True, edge)
        accumulate([1], (1, 2), True, False, edge)

    @pl.when(tm < n_tm - 1)
    def _():
        accumulate([fdev], (0, 1), True, False, edge)

    for hop in range(2, n_space - 1):
        token(hop)

    def corners_in(corners):
        @pl.when(space < n_space - 1)
        def _():
            corners[0].wait_recv()

        @pl.when(space > 0)
        def _():
            corners[1].wait_recv()

    @pl.when(tm > 0)
    def _():
        corners_in(forward_corners)
        forward[2].wait_recv()
        accumulate([1], (0,), False, True, range(hdev))

    @pl.when(tm < n_tm - 1)
    def _():
        back[2].wait_recv()
        accumulate([fdev], (2,), False, True, inner)
        corners_in(back_corners)
        accumulate([fdev], (2,), False, True, edge)

    halves = [jnp.sum(stats[i], axis=0, keepdims=True) for i in range(2)]
    gathered[me] = jnp.concatenate(halves, axis=0)

    def stat_copy(step):
        return pltpu.make_async_remote_copy(
            src_ref=gathered.at[me],
            dst_ref=gathered.at[me],
            send_sem=stat_send.at[step],
            recv_sem=stat_recv.at[me],
            device_id=at(lax.rem(me + step, n)),
            device_id_type=MESH,
        )

    def stat_arrival(step):
        sender = lax.rem(me + step, n)
        return pltpu.make_async_remote_copy(
            src_ref=gathered.at[sender],
            dst_ref=gathered.at[sender],
            send_sem=stat_send.at[step],
            recv_sem=stat_recv.at[sender],
            device_id=at(sender),
            device_id_type=MESH,
        )

    if n_space > 1:
        token(n_space - 1)

    @pl.loop(1, n)
    def _(step):
        stat_copy(step).start()

    @pl.when(tm < n_tm - 1)
    def _():
        dest_copy.wait_recv()

    @pl.when(tm == n_tm - 1)
    def _():
        next_ref[...] = jnp.zeros_like(next_ref)

    def numbers(shape, axis):
        return lax.broadcasted_iota(jnp.int32, shape, axis)

    along, across = numbers((held, held), 0), numbers((held, held), 1)
    source, column = numbers((rows, held), 0), numbers((rows, held), 1)
    named = jnp.dot(
        dest_ref[...].astype(jnp.float32),
        jnp.where(source == column, 1.0, 0.0),
        precision=lax.Precision.HIGHEST,
        preferred_element_type=jnp.float32,
    ) + jnp.dot(
        next_ref[...].astype(jnp.float32),
        jnp.where((source + rows == column) & (source < hdev), 1.0, 0.0),
        precision=lax.Precision.HIGHEST,
        preferred_element_type=jnp.float32,
    )
    wide_named = jnp.broadcast_to(named, (held, held))
    tall_named = jnp.sum(jnp.where(across == along, wide_named, 0.0), axis=1, keepdims=True)
    alike = (tall_named == wide_named) & (along < across) & ((along < rows) == (across < rows))
    rank = jnp.sum(jnp.where(alike, 1.0, 0.0), axis=0, keepdims=True)
    position = numbers((1, held), 1)
    here = (
        ((position < hdev) & first_tm)
        | ((position >= hdev) & (position < rows))
        | ((position >= rows) & (position < rows + hdev) & (~last_tm))
    )
    slot = named * slots_per + rank + jnp.where(position >= rows, 1.0 * own_slots, 0.0)
    slot = jnp.where(here, slot, -1.0)
    slots = numbers((place.shape[0], held), 0).astype(jnp.float32)
    place[...] = jnp.where(slots == slot, 1.0, 0.0).astype(jnp.bfloat16)

    @pl.loop(1, n)
    def _(step):
        stat_arrival(step).wait_recv()

    sums = jnp.sum(gathered[...], axis=0)
    position = lax.broadcasted_iota(jnp.int32, (2, chans), 1)
    per = chans // GROUPS
    reach = 1
    while reach < per:
        low = lax.rem(position // reach, 2) == 0
        sums = sums + jnp.where(
            low, pltpu.roll(sums, chans - reach, 1), pltpu.roll(sums, reach, 1)
        )
        reach *= 2
    amount = jnp.full((1, chans), 1, jnp.int32) * count
    total_count = amount.astype(jnp.float32) * (n_space * hdev * width * per)
    mean = sums[0:1] / total_count
    var = jnp.maximum(sums[1:2] / total_count - mean * mean, 0.0)
    scale = lax.rsqrt(var + 1e-06) * gain_ref[...]
    offset = shift_ref[...] - mean * scale
    scale, offset = 0.5 * scale, 0.5 * offset
    row = numbers((held, chans), 0)
    frame = jnp.zeros((held, chans), jnp.int32) + tm * fdev
    for f in range(1, fdev + 1):
        frame = frame + jnp.where(row >= f * hdev, 1, 0)
    frame_masks = jnp.where(frame < count, 1.0, 0.0)
    chunks = lat // (TILES * chans)

    wide_cells = TILES * chans

    def columns(chunk):
        return pl.ds(pl.multiple_of(chunk * wide_cells, wide_cells), wide_cells)

    def row_copies(chunk, step, sender):
        peer = lax.rem(tm + step, n_tm)
        place_of = peer if sender else tm
        return [
            pltpu.make_async_remote_copy(
                src_ref=source.at[peer, :, columns(chunk)],
                dst_ref=target.at[place_of, :, columns(chunk)],
                send_sem=send.at[chunk, step],
                recv_sem=recv.at[chunk, place_of],
                device_id={"tm": peer},
                device_id_type=MESH,
            )
            for source, target, send, recv in [
                (outgoing, out, row_send, row_recv),
                (extra, extra_in, extra_send, extra_recv),
            ]
        ]

    @functools.partial(lax.fori_loop, 0, chunks, init_val=None, unroll=True)
    def _(chunk, _carry):
        hidden = []
        for j in range(TILES):
            cells = []
            for i in range(folded):
                w = (chunk * TILES + j) * folded + i
                half = act[pl.ds(w, held, stride=pitch), :] * scale + offset
                cells.append((half + half * jnp.tanh(half)) * frame_masks)
            hidden.append(jnp.concatenate(cells, axis=1))
        hidden = jnp.concatenate(hidden, axis=0).astype(jnp.bfloat16)
        moments = (
            jnp.dot(hidden, wq[...], preferred_element_type=jnp.float32) + bias_ref[...]
        )
        wide = jnp.concatenate(
            [moments[j * held : (j + 1) * held] for j in range(TILES)], axis=1
        ).astype(jnp.bfloat16)
        routed = jnp.dot(place[...], wide, preferred_element_type=jnp.float32)
        for d in range(n_tm):
            start = d * slots_per
            outgoing[d, :, columns(chunk)] = routed[start : start + cap].astype(jnp.bfloat16)
            start = start + own_slots
            extra[d, :, columns(chunk)] = routed[start : start + capb].astype(jnp.bfloat16)

        @pl.loop(1, n_tm)
        def _(step):
            own, more = row_copies(chunk, step, False)
            own.start()

            @pl.when(tm < n_tm - 1)
            def _():
                more.start()

        mine = jnp.dot(
            place[pl.ds(pl.multiple_of(tm * slots_per, slots_per), slots_per), :],
            wide,
            preferred_element_type=jnp.float32,
        )
        out[tm, :, columns(chunk)] = mine[:cap].astype(jnp.bfloat16)
        extra_in[tm, :, columns(chunk)] = mine[own_slots : own_slots + capb].astype(
            jnp.bfloat16
        )

    @pl.loop(1, n)
    def _(step):
        stat_copy(step).wait_send()

    def sent(corners):
        @pl.when(space > 0)
        def _():
            corners[0].wait_send()

        @pl.when(space < n_space - 1)
        def _():
            corners[1].wait_send()

    @pl.when(tm < n_tm - 1)
    def _():
        for copy in forward:
            copy.wait_send()
        sent(back_corners)

    @pl.when(tm > 0)
    def _():
        for copy in back:
            copy.wait_send()
        dest_copy.wait_send()
        sent(forward_corners)

    @pl.when(space > 0)
    def _():
        early_rows[0].wait_send()
        late_rows[0].wait_send()

    @pl.when(space < n_space - 1)
    def _():
        early_rows[1].wait_send()
        late_rows[1].wait_send()

    @pl.loop(0, chunks)
    def _(chunk):
        @pl.loop(1, n_tm)
        def _(step):
            own, more = row_copies(chunk, step, False)
            own.wait_send()

            @pl.when(tm < n_tm - 1)
            def _():
                more.wait_send()

            own, more = row_copies(chunk, step, True)
            own.wait_recv()

            @pl.when(lax.rem(tm + step, n_tm) < n_tm - 1)
            def _():
                more.wait_recv()

        @pl.loop(1, n_tm)
        def _(t):
            out[t, :capb, columns(chunk)] = (
                out[t, :capb, columns(chunk)].astype(jnp.float32)
                + extra_in[t - 1, :, columns(chunk)].astype(jnp.float32)
            ).astype(jnp.bfloat16)


def hand_over(source, target, sem):
    copy = pltpu.make_async_copy(source, target, sem)
    copy.start()
    copy.wait()


def body(
    n_tm,
    n_space,
    video,
    frame_counts,
    conv_weight,
    norm_gain,
    norm_shift,
    quant_weight,
    quant_bias,
    row_dest,
):
    clips, fdev, hdev, width, chans = video.shape
    l2 = quant_weight.shape[1]
    rows = fdev * hdev
    lat = width * l2
    cap = min(max(2, 2 * rows // n_tm), rows)
    capb = min(cap, hdev)
    own_slots = -(-cap // 8) * 8
    slots_per = own_slots + -(-capb // 8) * 8
    held = -(-(rows + hdev) // 16) * 16
    pitch = width + 8
    n = n_tm * n_space
    chunks = lat // (TILES * chans)
    kept_bytes = n_tm * own_slots * lat * 2 + 128 * 1024
    hbm = pl.BlockSpec(memory_space=pltpu.HBM)
    out = pl.pallas_call(
        functools.partial(kernel, n_tm, n_space, cap, capb, own_slots, slots_per, pitch),
        out_shape=pltpu.VMEM((n_tm, cap, lat), jnp.bfloat16),
        in_specs=[hbm] * 8,
        out_specs=pl.BlockSpec(memory_space=pltpu.VMEM),
        scratch_shapes=[
            pltpu.VMEM((1, 1), jnp.int32),
            pltpu.VMEM((1, chans), jnp.float32),
            pltpu.VMEM((1, chans), jnp.float32),
            pltpu.VMEM((l2, chans), jnp.bfloat16),
            pltpu.VMEM((1, l2), jnp.float32),
            pltpu.VMEM((1, rows), jnp.int32),
            pltpu.VMEM((1, rows), jnp.int32),
            pltpu.VMEM((fdev + 2, hdev + 2, width, chans), jnp.bfloat16),
            pltpu.VMEM((3, 3, chans, 3 * chans), jnp.bfloat16),
            pltpu.VMEM((2, 3, chans, 3 * chans), jnp.bfloat16),
            pltpu.VMEM((held * pitch, chans), jnp.float32),
            pltpu.VMEM((chans // l2 * chans, chans), jnp.bfloat16),
            pltpu.VMEM((n_tm * slots_per, held), jnp.bfloat16),
            pltpu.VMEM((2, 8, chans), jnp.float32),
            pltpu.VMEM((n, 2, chans), jnp.float32),
            pltpu.VMEM((1, chans), jnp.float32),
            pltpu.VMEM((n_tm, cap, lat), jnp.bfloat16),
            pltpu.VMEM((n_tm, capb, lat), jnp.bfloat16),
            pltpu.VMEM((n_tm, capb, lat), jnp.bfloat16),
            pltpu.SemaphoreType.DMA((10,)),
            pltpu.SemaphoreType.DMA((15,)),
            pltpu.SemaphoreType.DMA((15,)),
            pltpu.SemaphoreType.DMA((n,)),
            pltpu.SemaphoreType.DMA((n,)),
            *[pltpu.SemaphoreType.DMA((chunks, n_tm))] * 4,
            pltpu.SemaphoreType.REGULAR((2,)),
        ],
        compiler_params=pltpu.CompilerParams(
            collective_id=0, has_side_effects=True, vmem_limit_bytes=VMEM - kept_bytes
        ),
    )(
        frame_counts.reshape(1, 1),
        video[0],
        conv_weight,
        norm_gain.reshape(1, chans),
        norm_shift.reshape(1, chans),
        quant_weight.T,
        quant_bias.reshape(1, l2),
        row_dest.reshape(1, rows),
    )
    return out.reshape(1, 1, 1, n_tm, cap, lat)


def solution(mesh):
    return jax.shard_map(
        functools.partial(body, mesh.shape["tm"], mesh.shape["space"]),
        mesh=mesh,
        in_specs=(
            P("clip", "tm", "space", None, None),
            P("clip"),
            P(),
            P(),
            P(),
            P(),
            P(),
            P("clip", "tm", "space", None, None),
        ),
        out_specs=P("clip", "tm", "space", None, None, None),
        check_vma=False,
    )
```

```python
import functools

import jax
import jax.numpy as jnp
from jax import lax
from jax.experimental import pallas as pl
from jax.experimental.pallas import tpu as pltpu
from jax.sharding import PartitionSpec as P

GROUPS = 32
MESH = pl.DeviceIdType.MESH
TILES = 10
VMEM = 64 * 1024 * 1024


def kernel(
    n_tm,
    n_space,
    cap,
    capb,
    own_slots,
    slots_per,
    pitch,
    count_hbm,
    video,
    weight,
    gain_hbm,
    shift_hbm,
    qw_hbm,
    qb_hbm,
    dest_hbm,
    out,
    count_ref,
    gain_ref,
    shift_ref,
    qw_ref,
    qb_ref,
    dest_ref,
    next_ref,
    xs,
    wb,
    folded_taps,
    act,
    wq,
    place,
    stats,
    gathered,
    bias_ref,
    outgoing,
    extra,
    extra_in,
    local_sem,
    halo_send,
    halo_recv,
    stat_send,
    stat_recv,
    row_send,
    row_recv,
    extra_send,
    extra_recv,
    token_sem,
):
    fdev, hdev, width, chans = video.shape
    l2 = qw_ref.shape[0]
    rows = fdev * hdev
    held = place.shape[1]
    folded = chans // l2
    lat = width * l2
    n = n_tm * n_space
    tm, space = lax.axis_index("tm"), lax.axis_index("space")
    me = tm * n_space + space
    first_tm, last_tm = tm == 0, tm == n_tm - 1

    def at(peer):
        return {"tm": peer // n_space, "space": lax.rem(peer, n_space)}

    barrier = pltpu.get_barrier_semaphore()

    near = n_tm == 2
    later = {"tm": lax.rem(tm + 1, n_tm)}
    earlier = {"tm": lax.rem(tm + n_tm - 1, n_tm)}
    above = {"space": lax.rem(space + n_space - 1, n_space)}
    below = {"space": lax.rem(space + 1, n_space)}

    def tell(sem, device):
        pl.semaphore_signal(sem, inc=1, device_id=device, device_id_type=MESH)

    if near:
        tell(barrier, later)

        @pl.when(space > 0)
        def _():
            tell(barrier, above)

        @pl.when(space < n_space - 1)
        def _():
            tell(barrier, below)

    else:

        @pl.loop(1, n)
        def _(step):
            tell(barrier, at(lax.rem(me + step, n)))

    taps = [
        pltpu.make_async_copy(
            weight.at[:, :, dw],
            wb.at[:, :, :, pl.ds(dw * chans, chans)],
            local_sem.at[1 + dw],
        )
        for dw in range(3)
    ]
    for tap in taps:
        tap.start()
    own = pltpu.make_async_copy(
        video, xs.at[pl.ds(1, fdev), pl.ds(1, hdev)], local_sem.at[0]
    )
    own.start()

    smalls = [
        pltpu.make_async_copy(src, dst, local_sem.at[4 + i])
        for i, (src, dst) in enumerate(
            [
                (qw_hbm, qw_ref),
                (qb_hbm, qb_ref),
                (dest_hbm, dest_ref),
                (gain_hbm, gain_ref),
                (shift_hbm, shift_ref),
                (count_hbm, count_ref),
            ]
        )
    ]
    for small in smalls:
        small.start()

    def prepare():
        zero_row = jnp.zeros((fdev + 2, width, chans), jnp.bfloat16)

        @pl.when(space == 0)
        def _():
            xs[:, 0] = zero_row

        @pl.when(space == n_space - 1)
        def _():
            xs[:, hdev + 1] = zero_row

        zero_frame = jnp.zeros((hdev * pitch, chans), jnp.float32)

        @pl.when(tm > 0)
        def _():
            act[pl.ds(0, hdev * pitch), :] = zero_frame

        @pl.when(tm == n_tm - 1)
        def _():
            act[pl.ds(rows * pitch, hdev * pitch), :] = zero_frame

        spare = held - rows - hdev
        act[pl.ds((rows + hdev) * pitch, spare * pitch), :] = jnp.zeros(
            (spare * pitch, chans), jnp.float32
        )

        for small in smalls:
            small.wait()
        lane = lax.broadcasted_iota(jnp.int32, (l2, chans), 1)
        sub = lax.broadcasted_iota(jnp.int32, (l2, chans), 0)
        spread = jnp.zeros((l2, chans), jnp.float32)
        for i in range(folded):
            pick = jnp.where(lane == sub + i * l2, 1.0, 0.0)
            spread = spread + pick
            wq[pl.ds(i * chans, chans), :] = lax.dot_general(
                qw_ref[...],
                pick.astype(jnp.bfloat16),
                (((0,), (0,)), ((), ())),
                preferred_element_type=jnp.float32,
            ).astype(jnp.bfloat16)
        bias_ref[...] = jnp.dot(
            qb_ref[...],
            spread,
            precision=lax.Precision.HIGHEST,
            preferred_element_type=jnp.float32,
        )
        stats[...] = jnp.zeros_like(stats)

    @pl.when(tm == 0)
    def _():
        prepare()

    if near:
        outer = (space == 0) | (space == n_space - 1)

        @pl.when(outer)
        def _():
            pl.semaphore_wait(barrier, min(n_space, 2))

        @pl.when(~outer)
        def _():
            pl.semaphore_wait(barrier, 3)

    else:
        pl.semaphore_wait(barrier, n - 1)

    def token(hop):
        if not near:
            return

        @pl.when(space == hop)
        def _():
            if hop > 0:
                pl.semaphore_wait(token_sem.at[0], 1)
            if hop < n_space - 1:
                tell(token_sem.at[0], below)

        @pl.when(space == n_space - 1 - hop)
        def _():
            if hop > 0:
                pl.semaphore_wait(token_sem.at[1], 1)
            if hop < n_space - 1:
                tell(token_sem.at[1], above)

    def remote(src, dst, index, device):
        return pltpu.make_async_remote_copy(
            src_ref=src,
            dst_ref=dst,
            send_sem=halo_send.at[index],
            recv_sem=halo_recv.at[index],
            device_id=device,
            device_id_type=MESH,
        )

    after = fdev + 1

    def frame_copies(source, target, index, device):
        return [
            remote(video.at[source, 0], xs.at[target, 1], index, device),
            remote(video.at[source, hdev - 1], xs.at[target, hdev], index + 1, device),
            remote(
                video.at[source, pl.ds(1, hdev - 2)],
                xs.at[target, pl.ds(2, hdev - 2)],
                index + 2,
                device,
            ),
        ]

    def corner_copies(target, index):
        return [
            remote(xs.at[target, 1], xs.at[target, hdev + 1], index, above),
            remote(xs.at[target, hdev], xs.at[target, 0], index + 1, below),
        ]

    forward = frame_copies(fdev - 1, 0, 0, later)
    back = frame_copies(0, after, 3, earlier)
    forward_corners = corner_copies(0, 6)
    back_corners = corner_copies(after, 8)
    half = fdev // 2

    def row_halo(start, count, index):
        source, target = pl.ds(start, count), pl.ds(start + 1, count)
        return [
            remote(video.at[source, 0], xs.at[target, hdev + 1], index, above),
            remote(video.at[source, hdev - 1], xs.at[target, 0], index + 1, below),
        ]

    early_rows, late_rows = row_halo(0, half, 10), row_halo(half, fdev - half, 13)
    dest_copy = remote(dest_hbm, next_ref, 12, earlier)

    second = lax.rem(lax.axis_index("clip"), 2) == 1

    def send_frames():
        @pl.when(tm > 0)
        def _():
            for copy in back:
                copy.start()

        @pl.when(tm < n_tm - 1)
        def _():
            for copy in forward:
                copy.start()

    def send_rows():
        @pl.when(space > 0)
        def _():
            early_rows[0].start()
            late_rows[0].start()

        @pl.when(space < n_space - 1)
        def _():
            early_rows[1].start()
            late_rows[1].start()

    @pl.when(~second)
    def _():
        send_rows()
        send_frames()

    @pl.when(second)
    def _():
        send_frames()
        send_rows()

    @pl.when(tm > 0)
    def _():
        dest_copy.start()

    token(0)

    @pl.when(tm > 0)
    def _():
        prepare()

    count = count_ref[...]

    def valid(frame):
        ids = jnp.full((1, chans), 0, jnp.int32) + (tm * fdev + frame)
        return jnp.where(ids < count, 1.0, 0.0)

    cell = lax.broadcasted_iota(jnp.int32, (width, chans), 0)

    def accumulate(fs, taps_of, fresh, final, hs):
        items = [(f, h) for f in fs for h in hs]
        m = len(items) * width

        def index(f, dt):
            p = f - 1 + dt
            return 1 if p == 0 and len(taps_of) == 3 else p

        if fs == [0]:
            frames_of = [[1], [1]]
            kernel_part = folded_taps[...].reshape(-1, 3 * chans)
        else:
            frames_of = [[index(f, dt) for f in fs] for dt in taps_of]
            kernel_part = wb[pl.ds(taps_of[0], len(taps_of))].reshape(-1, 3 * chans)
        pieces = [
            jnp.concatenate([xs[p, h + dh] for p in ps for h in hs], axis=0)
            for ps in frames_of
            for dh in range(3)
        ]
        y = jnp.dot(
            jnp.concatenate(pieces, axis=1), kernel_part, preferred_element_type=jnp.float32
        )
        for i, (f, h) in enumerate(items):
            part = y[i * width : (i + 1) * width]
            before = pltpu.roll(part[:, :chans], 1, 0)
            after_ = pltpu.roll(part[:, 2 * chans :], width - 1, 0)
            total = (
                part[:, chans : 2 * chans]
                + jnp.where(cell == 0, 0.0, before)
                + jnp.where(cell == width - 1, 0.0, after_)
            )
            spot = pl.ds((f * hdev + h) * pitch, width)
            if not fresh:
                total = total + act[spot, :]
            if final:
                total = total * valid(f)
                stats[0] += jnp.sum(total.reshape(width // 8, 8, chans), axis=0)
                stats[1] += jnp.sum((total * total).reshape(width // 8, 8, chans), axis=0)
            act[spot, :] = total

    inner, edge = list(range(1, hdev - 1)), [0, hdev - 1]

    @pl.when(tm == 0)
    def _():
        for tap in taps:
            tap.wait()

        @pl.loop(0, 3)
        def _(dh):
            total = sum(wb[dt, dh].astype(jnp.float32) for dt in range(3))
            high = total.astype(jnp.bfloat16)
            folded_taps[0, dh] = high
            folded_taps[1, dh] = (total - high.astype(jnp.float32)).astype(jnp.bfloat16)

    own.wait()

    @pl.when(tm > 0)
    def _():
        for tap in taps:
            tap.wait()

    def pass_corners(arrived, corners):
        arrived[0].wait_recv()
        arrived[1].wait_recv()

        @pl.when(space > 0)
        def _():
            corners[0].start()

        @pl.when(space < n_space - 1)
        def _():
            corners[1].start()

    @pl.when(tm == 0)
    def _():
        accumulate(range(1, fdev), (0, 1, 2), True, True, inner)
        accumulate([0], (0, 1, 2), True, True, inner)

    @pl.when(tm > 0)
    def _():
        accumulate(range(2, fdev), (0, 1, 2), True, True, inner)
        pass_corners(forward, forward_corners)
        accumulate([1], (1, 2), True, False, inner)

    @pl.when(tm < n_tm - 1)
    def _():
        pass_corners(back, back_corners)
        accumulate([fdev], (0, 1), True, False, inner)

    if n_space > 2:
        token(1)

    def rows_in(copies):
        @pl.when(space < n_space - 1)
        def _():
            copies[0].wait_recv()

        @pl.when(space > 0)
        def _():
            copies[1].wait_recv()

    rows_in(early_rows)

    @pl.when(tm == 0)
    def _():
        accumulate(range(1, half), (0, 1, 2), True, True, edge)
        accumulate([0], (0, 1, 2), True, True, edge)

    rows_in(late_rows)

    @pl.when(tm == 0)
    def _():
        accumulate(range(half, fdev), (0, 1, 2), True, True, edge)

    @pl.when(tm > 0)
    def _():
        accumulate(range(2, fdev), (0, 1, 2), True, True, edge)
        accumulate([1], (1, 2), True, False, edge)

    @pl.when(tm < n_tm - 1)
    def _():
        accumulate([fdev], (0, 1), True, False, edge)

    for hop in range(2, n_space - 1):
        token(hop)

    def corners_in(corners):
        @pl.when(space < n_space - 1)
        def _():
            corners[0].wait_recv()

        @pl.when(space > 0)
        def _():
            corners[1].wait_recv()

    @pl.when(tm > 0)
    def _():
        corners_in(forward_corners)
        forward[2].wait_recv()
        accumulate([1], (0,), False, True, range(hdev))

    @pl.when(tm < n_tm - 1)
    def _():
        back[2].wait_recv()
        accumulate([fdev], (2,), False, True, inner)
        corners_in(back_corners)
        accumulate([fdev], (2,), False, True, edge)

    halves = [jnp.sum(stats[i], axis=0, keepdims=True) for i in range(2)]
    gathered[me] = jnp.concatenate(halves, axis=0)

    def stat_copy(step):
        return pltpu.make_async_remote_copy(
            src_ref=gathered.at[me],
            dst_ref=gathered.at[me],
            send_sem=stat_send.at[step],
            recv_sem=stat_recv.at[me],
            device_id=at(lax.rem(me + step, n)),
            device_id_type=MESH,
        )

    def stat_arrival(step):
        sender = lax.rem(me + step, n)
        return pltpu.make_async_remote_copy(
            src_ref=gathered.at[sender],
            dst_ref=gathered.at[sender],
            send_sem=stat_send.at[step],
            recv_sem=stat_recv.at[sender],
            device_id=at(sender),
            device_id_type=MESH,
        )

    if n_space > 1:
        token(n_space - 1)

    @pl.loop(1, n)
    def _(step):
        stat_copy(step).start()

    @pl.when(tm < n_tm - 1)
    def _():
        dest_copy.wait_recv()

    @pl.when(tm == n_tm - 1)
    def _():
        next_ref[...] = jnp.zeros_like(next_ref)

    def numbers(shape, axis):
        return lax.broadcasted_iota(jnp.int32, shape, axis)

    along, across = numbers((held, held), 0), numbers((held, held), 1)
    source, column = numbers((rows, held), 0), numbers((rows, held), 1)
    named = jnp.dot(
        dest_ref[...].astype(jnp.float32),
        jnp.where(source == column, 1.0, 0.0),
        precision=lax.Precision.HIGHEST,
        preferred_element_type=jnp.float32,
    ) + jnp.dot(
        next_ref[...].astype(jnp.float32),
        jnp.where((source + rows == column) & (source < hdev), 1.0, 0.0),
        precision=lax.Precision.HIGHEST,
        preferred_element_type=jnp.float32,
    )
    wide_named = jnp.broadcast_to(named, (held, held))
    tall_named = jnp.sum(jnp.where(across == along, wide_named, 0.0), axis=1, keepdims=True)
    alike = (tall_named == wide_named) & (along < across) & ((along < rows) == (across < rows))
    rank = jnp.sum(jnp.where(alike, 1.0, 0.0), axis=0, keepdims=True)
    position = numbers((1, held), 1)
    here = (
        ((position < hdev) & first_tm)
        | ((position >= hdev) & (position < rows))
        | ((position >= rows) & (position < rows + hdev) & (~last_tm))
    )
    slot = named * slots_per + rank + jnp.where(position >= rows, 1.0 * own_slots, 0.0)
    slot = jnp.where(here, slot, -1.0)
    slots = numbers((place.shape[0], held), 0).astype(jnp.float32)
    place[...] = jnp.where(slots == slot, 1.0, 0.0).astype(jnp.bfloat16)

    @pl.loop(1, n)
    def _(step):
        stat_arrival(step).wait_recv()

    sums = jnp.sum(gathered[...], axis=0)
    position = lax.broadcasted_iota(jnp.int32, (2, chans), 1)
    per = chans // GROUPS
    reach = 1
    while reach < per:
        low = lax.rem(position // reach, 2) == 0
        sums = sums + jnp.where(
            low, pltpu.roll(sums, chans - reach, 1), pltpu.roll(sums, reach, 1)
        )
        reach *= 2
    amount = jnp.full((1, chans), 1, jnp.int32) * count
    total_count = amount.astype(jnp.float32) * (n_space * hdev * width * per)
    mean = sums[0:1] / total_count
    var = jnp.maximum(sums[1:2] / total_count - mean * mean, 0.0)
    scale = lax.rsqrt(var + 1e-06) * gain_ref[...]
    offset = shift_ref[...] - mean * scale
    scale, offset = 0.5 * scale, 0.5 * offset
    row = numbers((held, chans), 0)
    frame = jnp.zeros((held, chans), jnp.int32) + tm * fdev
    for f in range(1, fdev + 1):
        frame = frame + jnp.where(row >= f * hdev, 1, 0)
    frame_masks = jnp.where(frame < count, 1.0, 0.0)
    chunks = lat // (TILES * chans)

    wide_cells = TILES * chans

    def columns(chunk):
        return pl.ds(pl.multiple_of(chunk * wide_cells, wide_cells), wide_cells)

    def row_copies(chunk, step, sender):
        peer = lax.rem(tm + step, n_tm)
        place_of = peer if sender else tm
        return [
            pltpu.make_async_remote_copy(
                src_ref=source.at[peer, :, columns(chunk)],
                dst_ref=target.at[place_of, :, columns(chunk)],
                send_sem=send.at[chunk, step],
                recv_sem=recv.at[chunk, place_of],
                device_id={"tm": peer},
                device_id_type=MESH,
            )
            for source, target, send, recv in [
                (outgoing, out, row_send, row_recv),
                (extra, extra_in, extra_send, extra_recv),
            ]
        ]

    @functools.partial(lax.fori_loop, 0, chunks, init_val=None, unroll=True)
    def _(chunk, _carry):
        hidden = []
        for j in range(TILES):
            cells = []
            for i in range(folded):
                w = (chunk * TILES + j) * folded + i
                half = act[pl.ds(w, held, stride=pitch), :] * scale + offset
                cells.append((half + half * jnp.tanh(half)) * frame_masks)
            hidden.append(jnp.concatenate(cells, axis=1))
        hidden = jnp.concatenate(hidden, axis=0).astype(jnp.bfloat16)
        moments = (
            jnp.dot(hidden, wq[...], preferred_element_type=jnp.float32) + bias_ref[...]
        )
        wide = jnp.concatenate(
            [moments[j * held : (j + 1) * held] for j in range(TILES)], axis=1
        ).astype(jnp.bfloat16)
        routed = jnp.dot(place[...], wide, preferred_element_type=jnp.float32)
        for d in range(n_tm):
            start = d * slots_per
            outgoing[d, :, columns(chunk)] = routed[start : start + cap].astype(jnp.bfloat16)
            start = start + own_slots
            extra[d, :, columns(chunk)] = routed[start : start + capb].astype(jnp.bfloat16)

        @pl.loop(1, n_tm)
        def _(step):
            own, more = row_copies(chunk, step, False)
            own.start()

            @pl.when(tm < n_tm - 1)
            def _():
                more.start()

        mine = jnp.dot(
            place[pl.ds(pl.multiple_of(tm * slots_per, slots_per), slots_per), :],
            wide,
            preferred_element_type=jnp.float32,
        )
        out[tm, :, columns(chunk)] = mine[:cap].astype(jnp.bfloat16)
        extra_in[tm, :, columns(chunk)] = mine[own_slots : own_slots + capb].astype(
            jnp.bfloat16
        )

    @pl.loop(1, n)
    def _(step):
        stat_copy(step).wait_send()

    def sent(corners):
        @pl.when(space > 0)
        def _():
            corners[0].wait_send()

        @pl.when(space < n_space - 1)
        def _():
            corners[1].wait_send()

    @pl.when(tm < n_tm - 1)
    def _():
        for copy in forward:
            copy.wait_send()
        sent(back_corners)

    @pl.when(tm > 0)
    def _():
        for copy in back:
            copy.wait_send()
        dest_copy.wait_send()
        sent(forward_corners)

    @pl.when(space > 0)
    def _():
        early_rows[0].wait_send()
        late_rows[0].wait_send()

    @pl.when(space < n_space - 1)
    def _():
        early_rows[1].wait_send()
        late_rows[1].wait_send()

    @pl.loop(0, chunks)
    def _(chunk):
        @pl.loop(1, n_tm)
        def _(step):
            own, more = row_copies(chunk, step, False)
            own.wait_send()

            @pl.when(tm < n_tm - 1)
            def _():
                more.wait_send()

            own, more = row_copies(chunk, step, True)
            own.wait_recv()

            @pl.when(lax.rem(tm + step, n_tm) < n_tm - 1)
            def _():
                more.wait_recv()

        @pl.loop(1, n_tm)
        def _(t):
            out[t, :capb, columns(chunk)] = (
                out[t, :capb, columns(chunk)].astype(jnp.float32)
                + extra_in[t - 1, :, columns(chunk)].astype(jnp.float32)
            ).astype(jnp.bfloat16)


def hand_over(source, target, sem):
    copy = pltpu.make_async_copy(source, target, sem)
    copy.start()
    copy.wait()


def body(
    n_tm,
    n_space,
    video,
    frame_counts,
    conv_weight,
    norm_gain,
    norm_shift,
    quant_weight,
    quant_bias,
    row_dest,
):
    clips, fdev, hdev, width, chans = video.shape
    l2 = quant_weight.shape[1]
    rows = fdev * hdev
    lat = width * l2
    cap = min(max(2, 2 * rows // n_tm), rows)
    capb = min(cap, hdev)
    own_slots = -(-cap // 8) * 8
    slots_per = own_slots + -(-capb // 8) * 8
    held = -(-(rows + hdev) // 16) * 16
    pitch = width + 8
    n = n_tm * n_space
    chunks = lat // (TILES * chans)
    kept_bytes = n_tm * own_slots * lat * 2 + 128 * 1024
    hbm = pl.BlockSpec(memory_space=pltpu.HBM)
    out = pl.pallas_call(
        functools.partial(kernel, n_tm, n_space, cap, capb, own_slots, slots_per, pitch),
        out_shape=pltpu.VMEM((n_tm, cap, lat), jnp.bfloat16),
        in_specs=[hbm] * 8,
        out_specs=pl.BlockSpec(memory_space=pltpu.VMEM),
        scratch_shapes=[
            pltpu.VMEM((1, 1), jnp.int32),
            pltpu.VMEM((1, chans), jnp.float32),
            pltpu.VMEM((1, chans), jnp.float32),
            pltpu.VMEM((l2, chans), jnp.bfloat16),
            pltpu.VMEM((1, l2), jnp.float32),
            pltpu.VMEM((1, rows), jnp.int32),
            pltpu.VMEM((1, rows), jnp.int32),
            pltpu.VMEM((fdev + 2, hdev + 2, width, chans), jnp.bfloat16),
            pltpu.VMEM((3, 3, chans, 3 * chans), jnp.bfloat16),
            pltpu.VMEM((2, 3, chans, 3 * chans), jnp.bfloat16),
            pltpu.VMEM((held * pitch, chans), jnp.float32),
            pltpu.VMEM((chans // l2 * chans, chans), jnp.bfloat16),
            pltpu.VMEM((n_tm * slots_per, held), jnp.bfloat16),
            pltpu.VMEM((2, 8, chans), jnp.float32),
            pltpu.VMEM((n, 2, chans), jnp.float32),
            pltpu.VMEM((1, chans), jnp.float32),
            pltpu.VMEM((n_tm, cap, lat), jnp.bfloat16),
            pltpu.VMEM((n_tm, capb, lat), jnp.bfloat16),
            pltpu.VMEM((n_tm, capb, lat), jnp.bfloat16),
            pltpu.SemaphoreType.DMA((10,)),
            pltpu.SemaphoreType.DMA((15,)),
            pltpu.SemaphoreType.DMA((15,)),
            pltpu.SemaphoreType.DMA((n,)),
            pltpu.SemaphoreType.DMA((n,)),
            *[pltpu.SemaphoreType.DMA((chunks, n_tm))] * 4,
            pltpu.SemaphoreType.REGULAR((2,)),
        ],
        compiler_params=pltpu.CompilerParams(
            collective_id=0, has_side_effects=True, vmem_limit_bytes=VMEM - kept_bytes
        ),
    )(
        frame_counts.reshape(1, 1),
        video[0],
        conv_weight,
        norm_gain.reshape(1, chans),
        norm_shift.reshape(1, chans),
        quant_weight.T,
        quant_bias.reshape(1, l2),
        row_dest.reshape(1, rows),
    )
    return out.reshape(1, 1, 1, n_tm, cap, lat)


def solution(mesh):
    return jax.shard_map(
        functools.partial(body, mesh.shape["tm"], mesh.shape["space"]),
        mesh=mesh,
        in_specs=(
            P("clip", "tm", "space", None, None),
            P("clip"),
            P(),
            P(),
            P(),
            P(),
            P(),
            P("clip", "tm", "space", None, None),
        ),
        out_specs=P("clip", "tm", "space", None, None, None),
        check_vma=False,
    )
```
